512 devices in a mesh: gx: 8 (over x_hi, y), yz: 64 (over x_lo, z, core).
Axes of the slice: x: 4 (x_hi: 2, x_lo: 2; x = x_hi * 2 + x_lo), y: 4, z: 16, core: 2. Of those that a mesh axis runs over, the one named last changes fastest.
Arguments:
- old_pos: float32 [3, 131072], P(None, ('gx', 'yz')), may hold values from 0 to 1
- old_species: int32 [131072], P(('gx', 'yz')), may hold values from 0 to 4
- block_dest: int32 [1024, 1], P(('gx', 'yz')), may hold values from 0 to 2; in each aligned block of 2 rows (0 to 1, 2 to 3, ...) no two rows name the same one
- block_count: int32 [1024], P(('gx', 'yz')), may hold values from 1 to 128
- send_list: int32 [2048, 64], P(('gx', 'yz')), may hold values from 0 to 383
- neighbours: int32 [4, 196608], P(None, ('gx', 'yz')), may hold values from 0 to 639
- embed: float32 [5, 128], replicated, may hold values from -6 to 6
- atom_ref: float32 [5], replicated, may hold values from -3 to -0.5
- w_up: float32 [2, 128, 128], replicated, may hold values from -0.5 to 0.5
- gammas: float32 [2, 8], replicated, may hold values from 0.3 to 3
- w_rad: float32 [2, 8, 384], replicated, may hold values from -2 to 2
- w_mix: float32 [2, 128, 128], replicated, may hold values from -0.5 to 0.5
- readout: float32 [2, 128], replicated, may hold values from -0.5 to 0.5
Outputs:
- forces: float32 [3, 196608], P(None, ('gx', 'yz'))
- energy: float32 [], replicated
The draws below stay inside these ranges and needn't reach their ends.
Inputs may be any that keep to these rules, and one draw needn't show every extreme that they name: `block_dest`: 0 sends a block to the previous index along yz, 1 keeps it, 2 sends it to the next; among the 2 blocks of one brick at most 1 share a destination, and some destination has exactly 1. `send_list`: slots after migration; row f of a brick's four rows lists what it sends to face f of its neighbours (rows 0, 1 to the next and previous index along gx, rows 2, 3 to the next and previous along yz). `neighbours`: an entry below 384 is a slot of the brick; 384 + f * 64 + g is ghost g of face f.
All inputs are finite; a program needn't handle non-finite values.
Results may differ from the reference program's by a relative error of at most 0.0003.
Values sent between devices are 32-bit elements; how exact they have to be, the bound alone decides.
A program may use at most 64 MiB of HBM per device.

```python
import math
import jax
import jax.numpy as jnp
import numpy as np
from jax import lax

C = 128
NR = 8
SPEC = 5
LAYERS = 2
NE = 4
BLK = 128
NB = 2
MOST = 1
SL = 384
GH = 64
OLD_SLOTS = 131072
BLOCKS = 1024
SLOTS = 196608
LISTS = 2048
N_GX = 8
N_YZ = 64


def plant(values, stream_key, least, top_value):
    longest = values.shape.index(max(values.shape))
    spots = []
    for shift in (0, 1):
        where = [jax.random.randint(jax.random.fold_in(stream_key, axis), (), 0, length) for axis, length in enumerate(values.shape)]
        where[longest] = (where[longest] + shift) % values.shape[longest]
        spots.append(tuple(where))
    return values.at[spots[0]].set(least).at[spots[1]].set(top_value)


def steps_of(stream_key, shape, shards, low, high):
    gain = 1.0
    for dim, parts in shards:
        steps = jax.random.uniform(jax.random.fold_in(jax.random.fold_in(stream_key, 6), dim), (parts,), jnp.float32, low / len(shards), high / len(shards))
        gain = gain * jnp.repeat(jnp.exp(steps), shape[dim] // parts).reshape((-1,) + (1,) * (len(shape) - 1 - dim))
    return gain


def deal_out(stream_key, own, number, rows, count, top, reach, slope):
    order = jax.random.permutation(stream_key, count)
    heavy_load, common = load_shares(count, rows * top, reach, slope, True), load_shares(count, rows * top, reach, slope, False)
    places = jnp.arange(count)

    def named(lengths, rotation):
        used = int((lengths > 0).sum())
        fixed = max(1, used // 4)
        shifted = fixed + (places - fixed + rotation * (used - fixed)) % max(1, count - fixed)
        return jnp.zeros((count,), jnp.int32).at[order[jnp.where(places < fixed, places, shifted)]].set(jnp.asarray(lengths, jnp.int32))

    lengths = jnp.where(number % 4 == 0, named(heavy_load, number // 4), named(common, number - number // 4 - 1))
    mixed = jax.random.permutation(jax.random.fold_in(own, 3), count)
    donor, receiver = mixed[0:count // 2 * 2:2], mixed[1:count // 2 * 2:2]
    slack = jnp.minimum(lengths[donor] - 1, reach - lengths[receiver]) // 2
    slack = jnp.where((donor == order[0]) | (receiver == order[0]) | (lengths[receiver] == 0), 0, jnp.maximum(slack, 0))
    shifted = jax.random.randint(jax.random.fold_in(own, 4), (count // 2,), 0, 1 << 20) % (slack + 1)
    lengths = lengths.at[donor].add(-shifted).at[receiver].add(shifted)
    labels = jnp.searchsorted(jnp.cumsum(lengths), jnp.arange(rows * top), side="right").astype(jnp.int32)
    listing = labels.reshape(top, rows).T
    listing = listing[jax.random.permutation(jax.random.fold_in(own, 1), rows)]
    rotation = jax.random.randint(jax.random.fold_in(own, 2), (rows, 1), 0, top)
    return jnp.take_along_axis(listing, (jnp.arange(top)[None, :] + rotation) % top, axis=1)


def load_shares(count, total, bound, slope, full):
    loads = [(1 << 20) // math.isqrt(standing ** slope) + 1 for standing in range(1, count + 1)]
    largest = bound if full else min(bound, max(-(-total // count), total * loads[0] // sum(loads)))
    least = 1 if total - largest >= count - 1 else 0
    given, spare = [largest] + [least] * (count - 1), total - largest - least * (count - 1)
    while spare > 0:
        movable = [i for i in range(1, count) if given[i] < largest] or [i for i in range(1, count) if given[i] < bound]
        mass, left = sum([loads[i] for i in movable]), spare
        for i in movable:
            more = min(bound - given[i], max(1, left * loads[i] // mass), spare)
            given[i] = given[i] + more
            spare = spare - more
    return np.array(given)


def noise(own_key, dims, scale, limit, kind=jnp.bfloat16):
    return jnp.clip(scale * jax.random.normal(own_key, dims, jnp.float32), -limit, limit).astype(kind)


def setup_inputs(seed: int = 0) -> dict:
    arg_keys = jax.random.split(jax.random.key(seed), 14)
    old_pos = jnp.clip(1.0 * jax.random.uniform(arg_keys[0], (3, OLD_SLOTS), jnp.float32) ** steps_of(arg_keys[0], (3, OLD_SLOTS), ((1, 512),), -0.2, 0.2), 0.0, 1.0)
    old_species = plant(jax.random.randint(arg_keys[1], (OLD_SLOTS,), 0, SPEC), jax.random.fold_in(arg_keys[1], 1), 0, SPEC - 1).astype(jnp.int32)
    block_dest_keys = jax.random.split(jax.random.fold_in(arg_keys[2], 1), BLOCKS // NB)
    block_dest_turns = jax.random.permutation(jax.random.fold_in(arg_keys[2], 3), BLOCKS // NB)
    block_dest = jax.vmap(lambda own, number: deal_out(jax.random.fold_in(arg_keys[2], 2), own, number, NB, 3, 1, MOST, 1))(block_dest_keys, block_dest_turns).reshape((BLOCKS, 1))
    block_count = plant(jax.random.randint(arg_keys[3], (BLOCKS,), 1, BLK + 1), jax.random.fold_in(arg_keys[3], 1), 1, BLK).astype(jnp.int32)
    send_list = plant(jax.random.randint(arg_keys[4], (LISTS, GH), 0, SL), jax.random.fold_in(arg_keys[4], 1), 0, SL - 1).astype(jnp.int32)
    neighbours = plant(jax.random.randint(arg_keys[5], (NE, SLOTS), 0, SL + 4 * GH), jax.random.fold_in(arg_keys[5], 1), 0, (SL + 4 * GH) - 1).astype(jnp.int32)
    embed = noise(arg_keys[6], (SPEC, C), 1.0, 6.0, jnp.float32)
    atom_ref = jnp.clip(jax.random.uniform(arg_keys[7], (SPEC,), jnp.float32, -3.0, -0.5), -3.0, -0.5)
    w_up = noise(arg_keys[8], (LAYERS, C, C), C ** -0.5, 0.5, jnp.float32)
    gammas = jnp.clip(jnp.exp(jax.random.uniform(arg_keys[9], (LAYERS, NR), jnp.float32, math.log(0.3), math.log(3.0))), 0.3, 3.0)
    w_rad = noise(arg_keys[10], (LAYERS, NR, 3 * C), NR ** -0.5, 2.0, jnp.float32)
    w_mix = noise(arg_keys[11], (LAYERS, C, C), C ** -0.5, 0.5, jnp.float32)
    readout = noise(arg_keys[12], (LAYERS, C), C ** -0.5, 0.5, jnp.float32)
    return {"old_pos": old_pos, "old_species": old_species, "block_dest": block_dest, "block_count": block_count, "send_list": send_list, "neighbours": neighbours, "embed": embed, "atom_ref": atom_ref, "w_up": w_up, "gammas": gammas, "w_rad": w_rad, "w_mix": w_mix, "readout": readout}


root_three = math.sqrt(3.0)
root_fifteen = math.sqrt(15.0)
root_five_half = 0.5 * math.sqrt(5.0)
root_fifteen_half = 0.5 * math.sqrt(15.0)
degree_of = (0, 1, 1, 1, 2, 2, 2, 2, 2)
highest = lax.Precision.HIGHEST

def harmonics(unit_x, unit_y, unit_z):
    square = unit_x * unit_x + unit_y * unit_y + unit_z * unit_z
    return jnp.stack([jnp.ones_like(unit_x), root_three * unit_x, root_three * unit_y, root_three * unit_z, root_fifteen * unit_x * unit_y, root_fifteen * unit_y * unit_z, root_five_half * (3.0 * unit_z * unit_z - square), root_fifteen * unit_x * unit_z, root_fifteen_half * (unit_x * unit_x - unit_y * unit_y)], axis=1)

def edge_terms(source_pos, target_pos, source_feat, gammas, w_rad):
    offset = source_pos - target_pos
    length_sq = lax.optimization_barrier(jnp.sum(offset * offset, axis=0))
    basis = jnp.exp(-gammas[:, None] * length_sq[None, :])
    radial = jnp.einsum('qs,qf->sf', basis, w_rad, precision=highest)
    channels = source_feat.shape[1]
    radial = radial.reshape(-1, 3, channels)[:, jnp.asarray(degree_of, dtype=jnp.int32), :]
    scale = lax.rsqrt(1.0 + length_sq)
    unit = offset * scale[None, :]
    angular = harmonics(unit[0], unit[1], unit[2])
    return radial * angular[:, :, None] * source_feat[:, None, :]

def gather_messages(pos_ext, projected, neighbours, gammas, w_rad):
    slots = neighbours.shape[1]
    target_pos = pos_ext[:, :slots]

    def add_edges(column, total):
        source = neighbours[column]
        return total + edge_terms(pos_ext[:, source], target_pos, projected[source], gammas, w_rad)
    start = jnp.zeros((slots, 9, projected.shape[1]), pos_ext.dtype)
    return lax.fori_loop(0, neighbours.shape[0], add_edges, start)

def update(h_local, summed, live, w_mix, entries):
    averaged = summed / entries
    invariant = averaged[:, 0, :] + lax.optimization_barrier(jnp.sum(averaged[:, 1:4, :] * averaged[:, 1:4, :], axis=1)) + lax.optimization_barrier(jnp.sum(averaged[:, 4:, :] * averaged[:, 4:, :], axis=1))
    mixed = jnp.dot(invariant, w_mix, precision=highest)
    return (h_local + jax.nn.silu(mixed)) * live[:, None]

def layer_forward(pos_ext, h_ext, neighbours, live, w_up, gammas, w_rad, w_mix):
    projected = jnp.dot(h_ext, w_up, precision=highest)
    summed = gather_messages(pos_ext, projected, neighbours, gammas, w_rad)
    return update(h_ext[:neighbours.shape[1]], summed, live, w_mix, neighbours.shape[0])

def species_onehot(species, width, dtype):
    return (species[:, None] == jnp.arange(width, dtype=jnp.int32)[None, :]).astype(dtype)

def embed_rows(species, live, embed):
    onehot = species_onehot(species, embed.shape[0], embed.dtype)
    return jnp.dot(onehot, embed, precision=highest) * live[:, None]

def base_energy(species, live, atom_ref):
    onehot = species_onehot(species, atom_ref.shape[0], atom_ref.dtype)
    return jnp.dot(onehot, atom_ref, precision=highest) * live

def pack_blocks(old_pos, old_species, dest, count):
    n_blocks = dest.shape[0]
    per_block = old_species.shape[0] // n_blocks
    capacity = n_blocks // 2
    order = jnp.arange(n_blocks, dtype=jnp.int32)
    earlier = (order[:, None] > order[None, :]).astype(jnp.int32)
    same_dest = (dest[:, None] == dest[None, :]).astype(jnp.int32)
    rank = lax.optimization_barrier(jnp.sum(earlier * same_dest, axis=1))
    select = ((dest[None, None, :] == jnp.arange(3, dtype=jnp.int32)[:, None, None]) & (rank[None, None, :] == jnp.arange(capacity, dtype=jnp.int32)[None, :, None])).astype(jnp.int32)
    blocks_pos = old_pos.reshape(3, n_blocks, per_block)
    packed_pos = lax.optimization_barrier(jnp.sum(select.astype(old_pos.dtype)[:, :, None, :, None] * blocks_pos[None, None, :, :, :], axis=3))
    packed_species = lax.optimization_barrier(jnp.sum(select[:, :, :, None] * old_species.reshape(n_blocks, per_block)[None, None, :, :], axis=2))
    packed_count = lax.optimization_barrier(jnp.sum(select * count[None, None, :], axis=2))
    return (packed_pos, packed_species, packed_count)

def extend(rows, lists):
    picked = jax.vmap(jax.vmap(lambda table, chosen: table[chosen]))(rows, lists)
    faces = [jnp.roll(picked[:, :, 0], 1, axis=0), jnp.roll(picked[:, :, 1], -1, axis=0), jnp.roll(picked[:, :, 2], 1, axis=1), jnp.roll(picked[:, :, 3], -1, axis=1)]
    ghosts = jnp.stack(faces, axis=2).reshape(rows.shape[0], rows.shape[1], -1, rows.shape[3])
    return jnp.concatenate([rows, ghosts], axis=2)

def reference(old_pos, old_species, block_dest, block_count, send_list, neighbours, embed, atom_ref, w_up, gammas, w_rad, w_mix, readout):
    grid_x = N_GX
    grid_yz = N_YZ
    devices = grid_x * grid_yz
    pos_dev = old_pos.reshape(3, devices, -1).transpose(1, 0, 2)
    species_dev = old_species.reshape(devices, -1)
    dest_dev = block_dest.reshape(devices, -1)
    count_dev = block_count.reshape(devices, -1)
    packed_pos, packed_species, packed_count = jax.vmap(pack_blocks)(pos_dev, species_dev, dest_dev, count_dev)

    def arrive(packed):
        packed = packed.reshape((grid_x, grid_yz) + packed.shape[1:])
        return jnp.stack([jnp.roll(packed[:, :, group], group - 1, axis=1) for group in range(3)], axis=2)
    positions = arrive(packed_pos).transpose(0, 1, 4, 2, 3, 5).reshape(grid_x, grid_yz, 3, -1)
    species = arrive(packed_species).reshape(grid_x, grid_yz, -1)
    counts = arrive(packed_count).reshape(grid_x, grid_yz, -1)
    live = (jnp.arange(BLK, dtype=jnp.int32)[None, None, None, :] < counts[..., None]).astype(jnp.float32).reshape(grid_x, grid_yz, -1)
    slots = species.shape[2]
    lists = send_list.reshape(grid_x, grid_yz, 4, -1)
    edges = neighbours.reshape(NE, grid_x, grid_yz, slots).transpose(1, 2, 0, 3).reshape(devices, NE, slots)
    flat_live = live.reshape(devices, slots)
    per_device = jax.vmap(jax.vmap(embed_rows, in_axes=(0, 0, None)), in_axes=(0, 0, None))
    h_zero = per_device(species, live, embed)
    base = jax.vmap(jax.vmap(base_energy, in_axes=(0, 0, None)), in_axes=(0, 0, None))(species, live, atom_ref)

    def run_layer(layer, pos_ext, h_ext):

        def single(operands):
            return layer_forward(operands[0], operands[1], operands[2], operands[3], w_up[layer], gammas[layer], w_rad[layer], w_mix[layer])
        result = lax.map(jax.checkpoint(single), (pos_ext.reshape(devices, 3, -1), h_ext.reshape(devices, -1, h_ext.shape[-1]), edges, flat_live))
        return result.reshape(grid_x, grid_yz, slots, -1)

    def total_energy(coords):
        pos_ext = extend(coords.transpose(0, 1, 3, 2), lists).transpose(0, 1, 3, 2)
        h_one = run_layer(0, pos_ext, extend(h_zero, lists))
        h_two = run_layer(1, pos_ext, extend(h_one, lists))
        atomic = jnp.einsum('gysc,c->gys', h_one, readout[0], precision=highest) + jnp.einsum('gysc,c->gys', h_two, readout[1], precision=highest)
        return jnp.sum(base + live * atomic)
    total, grads = jax.value_and_grad(total_energy)(positions)
    energy = total / jnp.sum(live)
    forces = -grads.transpose(2, 0, 1, 3).reshape(3, -1)
    return (forces, energy)
```

```python
import math

import jax
import jax.numpy as jnp
from jax import lax
from jax.experimental import pallas as pl
from jax.experimental.pallas import tpu as pltpu
from jax.sharding import PartitionSpec as P

MESH = pl.DeviceIdType.MESH
F32 = jnp.float32
BF16 = jnp.bfloat16

R3 = math.sqrt(3.0)
R15 = math.sqrt(15.0)
R5 = math.sqrt(5.0)
DEGREE = (0, 1, 1, 1, 2, 2, 2, 2, 2)

C = 128
NE = 4
BLK = 128
SL = 384
GH = 64
NG = 4 * GH
EXT = SL + NG
E = NE * SL
NN = (((1,), (0,)), ((), ()))
NT = (((1,), (1,)), ((), ()))
TN = (((0,), (0,)), ((), ()))


def dot(a, b, dims=NN):
    return lax.dot_general(a, b, dims, preferred_element_type=F32)


def head(x):
    return x.astype(BF16).astype(F32)


def parts2(x):
    hi = x.astype(BF16)
    return hi, (x - hi.astype(F32)).astype(BF16)


def stack3(x):
    hi = head(x)
    mid = head(x - hi)
    return jnp.concatenate([hi, mid, x - hi - mid], axis=0).astype(BF16)


def fold3(x):
    return x[0:8] + x[8:16] + x[16:24]


def weight_lhs(w):
    hi, lo = parts2(w)
    return jnp.concatenate([hi, hi, lo], axis=1)


def weight_dot(lhs, x, dims=NN):
    hi, lo = parts2(x)
    return dot(lhs, jnp.concatenate([hi, lo, hi], axis=0 if dims is NN else 1), dims)


def body(
    pos_in, species_in, dest_in, count_in, list_in, near_in, embed_in, atom_in, up_in, gamma_in,
    rad_in, mix_in, read_in,
    force_out, energy_out,
    tile_ref, mig_send, mig_recv, a_ref, tail_ref, gsend, grecv, emb_ref,
    oh_ref, soh_ref, y_ref, r_ref, rp_ref, p_ref, gp_ref, acc_ref, b_ref, gb_ref,
    psend, precv, bsend, brecv, fsend, frecv, gy_ref, send_sem, recv_sem,
):
    gx, yz = lax.axis_index("gx"), lax.axis_index("yz")
    n_gx, n_yz = lax.axis_size("gx"), lax.axis_size("yz")
    xp = (lax.rem(gx + 1, n_gx), yz)
    xm = (lax.rem(gx + n_gx - 1, n_gx), yz)
    yp = (gx, lax.rem(yz + 1, n_yz))
    ym = (gx, lax.rem(yz + n_yz - 1, n_yz))

    barrier = pltpu.get_barrier_semaphore()
    for there in (xp, xm, yp, ym):
        pl.semaphore_signal(barrier, inc=1, device_id=there, device_id_type=MESH)

    def copy(src, dst, number, there):
        return pltpu.make_async_remote_copy(
            src_ref=src, dst_ref=dst, send_sem=send_sem.at[number], recv_sem=recv_sem.at[number],
            device_id=there, device_id_type=MESH,
        )

    sub = lax.broadcasted_iota(jnp.int32, (8, 128), 0)
    lane = lax.broadcasted_iota(jnp.int32, (8, 128), 1)

    for b in range(2):
        kinds = jnp.broadcast_to(species_in[b * BLK:(b + 1) * BLK].reshape(1, BLK), (8, BLK))
        here = (kinds == sub - 3) & (lane < count_in[b])
        tile_ref[:, b * BLK:(b + 1) * BLK] = jnp.where(here, 1.0, 0.0).astype(F32)
    tile_ref[0:3, :] = pos_in[...]
    first, second = tile_ref[:, 0:BLK], tile_ref[:, BLK:2 * BLK]

    def packed(d):
        return jnp.where(dest_in[0, 0] == d, first, jnp.where(dest_in[1, 0] == d, second, 0.0))

    mig_send[0] = packed(0)
    mig_send[1] = packed(2)
    a_ref[:, BLK:2 * BLK] = packed(1)
    pl.semaphore_wait(barrier, 4)
    moves = [copy(mig_send.at[0], mig_recv.at[0], 0, ym), copy(mig_send.at[1], mig_recv.at[1], 1, yp)]
    for move in moves:
        move.start()

    for pair in range(2):
        row = jnp.concatenate([list_in[2 * pair:2 * pair + 1, :], list_in[2 * pair + 1:2 * pair + 2, :]], axis=1)
        at = lax.broadcasted_iota(jnp.int32, (SL, 128), 0)
        soh_ref[:, pair * 128:(pair + 1) * 128] = jnp.where(at == row, 1.0, 0.0).astype(BF16)
    for k in range(NE):
        row = near_in[k:k + 1, :]

        def fill(block, _, row=row, k=k):
            base = pl.multiple_of(block * 128, 128)
            at = lax.broadcasted_iota(jnp.int32, (128, SL), 0) + base
            oh_ref[pl.ds(base, 128), k * SL:(k + 1) * SL] = jnp.where(at == row, 1.0, 0.0).astype(BF16)
            return 0

        lax.fori_loop(0, EXT // 128, fill, 0)

    emb_ref[...] = jnp.zeros((8, C), F32)
    emb_ref[3:8, :] = embed_in[...]
    emb24 = stack3(emb_ref[...])
    table24 = stack3(weight_dot(weight_lhs(emb_ref[...]), up_in[0]))
    mix_t = [weight_lhs(mix_in[t].T) for t in range(2)]
    mix_n = [weight_lhs(mix_in[t]) for t in range(2)]
    up1_t = weight_lhs(up_in[1].T)
    up1_n = weight_lhs(up_in[1])
    reads = jnp.concatenate([read_in[...], jnp.zeros((6, C), F32)], axis=0).T
    read_col = [jnp.broadcast_to(reads[:, t:t + 1], (C, SL)) for t in range(2)]
    rad24 = []
    for t in range(2):
        hi = head(rad_in[t])
        rad24.append(jnp.concatenate([hi, hi, rad_in[t] - hi], axis=0).astype(BF16))

    def column(values):
        out = jnp.zeros((8, 128), F32)
        for q in range(len(values)):
            if values[q] is not None:
                out = jnp.where(sub == q, values[q], out)
        return out

    gamma_col = [column([gamma_in[t, q] for q in range(8)]) for t in range(2)]
    atom_col = column([None, None, None] + [atom_in[q] for q in range(5)])

    for move in moves:
        move.wait()
    a_ref[:, 0:BLK] = mig_recv[0]
    a_ref[:, 2 * BLK:3 * BLK] = mig_recv[1]

    atoms = a_ref[...]
    atoms24 = stack3(atoms)
    picked = fold3(dot(atoms24, soh_ref[...]))
    gsend[0] = picked[:, 0:128]
    gsend[1] = picked[:, 128:256]
    ghosts = [copy(gsend.at[f // 2], grecv.at[f], 2 + f, (xp, xm, yp, ym)[f]) for f in range(4)]
    for ghost in ghosts:
        ghost.start()

    row_of = lax.broadcasted_iota(jnp.int32, (8, SL), 0)
    marks = jnp.where(row_of >= 3, atoms, 0.0)
    live = jnp.sum(marks, axis=0, keepdims=True)
    marks24 = jnp.concatenate([marks, marks, marks], axis=0).astype(BF16)
    h0 = dot(emb24, marks24, TN)
    near_local = fold3(dot(atoms24, oh_ref[0:SL, :]))

    for ghost in ghosts:
        ghost.wait()
    low = lane < GH
    ghost8 = jnp.concatenate([jnp.where(low, grecv[0], grecv[1]), jnp.where(low, grecv[2], grecv[3])], axis=1)
    near = near_local + fold3(dot(stack3(ghost8), oh_ref[SL:EXT, :]))

    def spread(rows, d):
        return jnp.broadcast_to(rows[d:d + 1, :], (8, rows.shape[1]))

    def offsets():
        out = []
        for d in range(3):
            there = spread(atoms, d)
            out.append(spread(near, d) - jnp.concatenate([there] * NE, axis=1))
        return out

    rx, ry, rz = offsets()
    sq = rx * rx + ry * ry + rz * rz
    inv = lax.rsqrt(1.0 + sq)
    ux, uy, uz = rx * inv, ry * inv, rz * inv
    y_ref[0] = R3 * ux
    y_ref[1] = R3 * uy
    y_ref[2] = R3 * uz
    y_ref[3] = R15 * ux * uy
    y_ref[4] = R15 * uy * uz
    y_ref[5] = (0.5 * R5) * (2.0 * uz * uz - ux * ux - uy * uy)
    y_ref[6] = R15 * ux * uz
    y_ref[7] = (0.5 * R15) * (ux * ux - uy * uy)
    for d, value in enumerate((rx, ry, rz, sq)):
        tail_ref[d] = value

    def basis(t):
        cols = jnp.concatenate([gamma_col[t]] * (E // 128), axis=1)
        return cols, 0.25 * jnp.exp(-cols * tail_ref[3])

    def radial(t, values, out_ref):
        hi = head(values)
        rows = jnp.concatenate([hi, values - hi, hi], axis=0).astype(BF16)
        for l in range(3):
            out_ref[t, l] = dot(rad24[t][:, l * C:(l + 1) * C], rows, TN)

    cols0, basis0 = basis(0)
    radial(0, basis0, r_ref)
    near_marks = jnp.where(lax.broadcasted_iota(jnp.int32, (8, E), 0) >= 3, near, 0.0)
    p_ref[0] = dot(table24, jnp.concatenate([near_marks] * 3, axis=0).astype(BF16), TN)

    def forward(t):
        def step(cb, _):
            r = pl.ds(pl.multiple_of(cb * 8, 8), 8)
            for lt in range(3):
                acc = [None] * 9
                for k in range(NE):
                    e = pl.ds(k * SL + lt * 128, 128)
                    p = p_ref[t, r, e]
                    terms = [r_ref[t, l, r, e] * p for l in range(3)]
                    for m in range(9):
                        value = terms[DEGREE[m]]
                        if m:
                            value = value * y_ref[m - 1, :, e]
                        acc[m] = value if acc[m] is None else acc[m] + value
                i = pl.ds(lt * 128, 128)
                total = acc[0]
                for m in range(1, 9):
                    acc_ref[t, m - 1, r, i] = acc[m]
                    total = total + acc[m] * acc[m]
                b_ref[r, i] = total
            return 0

        lax.fori_loop(0, C // 8, step, 0)
        mixed = weight_dot(mix_t[t], b_ref[...])
        return mixed, 1.0 / (1.0 + jnp.exp(-mixed))

    mixed0, gate0 = forward(0)
    h1 = live * (h0 + mixed0 * gate0)
    slope0 = live * (gate0 * (1.0 + mixed0 * (1.0 - gate0)))

    p1 = weight_dot(up1_t, h1)
    p1_parts = jnp.concatenate(parts2(p1), axis=0)
    sent = dot(p1_parts, soh_ref[...])
    psend[...] = (sent[0:C] + sent[C:2 * C]).T
    faces = [pl.ds(f * GH, GH) for f in range(4)]
    outs = [copy(psend.at[faces[f]], precv.at[faces[f]], 6 + f, (xp, xm, yp, ym)[f]) for f in range(4)]
    for out in outs:
        out.start()

    cols1, basis1 = basis(1)
    radial(1, basis1, r_ref)
    radial(1, -cols1 * basis1, rp_ref)
    radial(0, -cols0 * basis0, rp_ref)
    local1 = dot(p1_parts, oh_ref[0:SL, :])
    p_ref[1] = local1[0:C] + local1[C:2 * C]

    for out in outs:
        out.wait()
    ghost1 = dot(jnp.concatenate(parts2(precv[...].T), axis=0), oh_ref[SL:EXT, :])
    p_ref[1] = p_ref[1] + (ghost1[0:C] + ghost1[C:2 * C])

    mixed1, gate1 = forward(1)
    h2 = live * (h1 + mixed1 * gate1)
    value = h1 * read_col[0] + h2 * read_col[1]
    rows = jnp.sum(value, axis=0, keepdims=True)
    cols3 = jnp.concatenate([atom_col] * 3, axis=1)
    rows = rows + jnp.sum(marks * cols3, axis=0, keepdims=True)
    row_e = rows[:, 0:128] + rows[:, 128:256] + rows[:, 256:384]
    row_n = live[:, 0:128] + live[:, 128:256] + live[:, 256:384]
    energy_out[...] = jnp.where(sub == 0, row_e, jnp.where(sub == 1, row_n, 0.0))

    def backward(t):
        for lt in range(3):
            i = pl.ds(lt * 128, 128)
            for pair in range(2):
                edges = [pl.ds((2 * pair + kk) * SL + lt * 128, 128) for kk in range(2)]

                def step(cb, carry, i=i, edges=edges):
                    r = pl.ds(pl.multiple_of(cb * 8, 8), 8)
                    carry = list(carry)
                    g0 = gb_ref[r, i]
                    g = [g0] + [acc_ref[t, m, r, i] * (g0 + g0) for m in range(8)]
                    for kk, e in enumerate(edges):
                        p = p_ref[t, r, e]
                        y = [y_ref[m, :, e] for m in range(8)]
                        s1 = g[1] * y[0] + g[2] * y[1] + g[3] * y[2]
                        s2 = g[4] * y[3] + g[5] * y[4] + g[6] * y[5] + g[7] * y[6] + g[8] * y[7]
                        radial1, radial2 = r_ref[t, 1, r, e], r_ref[t, 2, r, e]
                        if t:
                            gp_ref[r, e] = r_ref[t, 0, r, e] * g0 + radial1 * s1 + radial2 * s2
                        slope = rp_ref[t, 0, r, e] * g0 + rp_ref[t, 1, r, e] * s1 + rp_ref[t, 2, r, e] * s2
                        t1, t2 = radial1 * p, radial2 * p
                        at = kk * 9
                        for m in range(8):
                            carry[at + m] = carry[at + m] + g[m + 1] * (t1 if m < 3 else t2)
                        carry[at + 8] = carry[at + 8] + p * slope
                    return tuple(carry)

                if t:
                    init = tuple(jnp.zeros((8, 128), F32) for _ in range(18))
                else:
                    init = tuple(gy_ref[m, :, e] for e in edges for m in range(9))
                done = lax.fori_loop(0, C // 8, step, init)
                for kk, e in enumerate(edges):
                    for m in range(9):
                        gy_ref[m, :, e] = done[kk * 9 + m]

    slope1 = live * (gate1 * (1.0 + mixed1 * (1.0 - gate1)))
    gb_ref[...] = weight_dot(mix_n[1], slope1 * read_col[1])
    backward(1)

    gp_parts = jnp.concatenate(parts2(gp_ref[...]), axis=0)
    back = dot(oh_ref[SL:EXT, :], gp_parts, NT)
    bsend[...] = back[:, 0:C] + back[:, C:2 * C]
    returns = [copy(bsend.at[faces[f]], brecv.at[faces[f]], 10 + f, (xm, xp, ym, yp)[f]) for f in range(4)]
    for item in returns:
        item.start()
    stay = dot(oh_ref[0:SL, :], gp_parts, NT)
    g_p = stay[:, 0:C] + stay[:, C:2 * C]
    for item in returns:
        item.wait()
    came = dot(soh_ref[...], jnp.concatenate(parts2(brecv[...]), axis=1))
    g_p = g_p + (came[:, 0:C] + came[:, C:2 * C])
    g_h1 = weight_dot(up1_n, g_p, NT) + (read_col[0] + read_col[1])
    gb_ref[...] = weight_dot(mix_n[0], slope0 * g_h1)
    backward(0)

    def summed(m):
        return jnp.sum(gy_ref[m], axis=0, keepdims=True)

    g1, g2, g3, g4, g5, g6, g7, g8 = [summed(m) for m in range(8)]
    g_sq = summed(8)
    rx, ry, rz, sq = [tail_ref[d][0:1, :] for d in range(4)]
    inv = lax.rsqrt(1.0 + sq)
    ux, uy, uz = rx * inv, ry * inv, rz * inv
    gux = R3 * g1 + R15 * (uy * g4 + uz * g7 + ux * g8) - R5 * (ux * g6)
    guy = R3 * g2 + R15 * (ux * g4 + uz * g5 - uy * g8) - R5 * (uy * g6)
    guz = R3 * g3 + R15 * (uy * g5 + ux * g7) + (2.0 * R5) * (uz * g6)
    twice = 2.0 * g_sq - (gux * rx + guy * ry + guz * rz) * (inv * inv * inv)
    g_edge = [gux * inv + twice * rx, guy * inv + twice * ry, guz * inv + twice * rz]
    row8 = lax.broadcasted_iota(jnp.int32, (8, E), 0)
    edge8 = jnp.where(row8 == 0, g_edge[0], jnp.where(row8 == 1, g_edge[1], jnp.where(row8 == 2, g_edge[2], 0.0)))
    edge24 = stack3(edge8)
    away = fold3(dot(edge24, oh_ref[SL:EXT, :], NT))
    fsend[0] = away[:, 0:128]
    fsend[1] = away[:, 128:256]
    lasts = [copy(fsend.at[f // 2], frecv.at[f], 14 + f, (xm, xp, ym, yp)[f]) for f in range(4)]
    for item in lasts:
        item.start()
    own = fold3(dot(edge24, oh_ref[0:SL, :], NT))
    for k in range(NE):
        own = own - edge8[:, k * SL:(k + 1) * SL]
    for item in lasts:
        item.wait()
    back8 = jnp.concatenate([jnp.where(low, frecv[0], frecv[1]), jnp.where(low, frecv[2], frecv[3])], axis=1)
    own = own + fold3(dot(stack3(back8), soh_ref[...], NT))
    force_out[...] = -own[0:3, :]


def shards(old_pos, old_species, block_dest, block_count, send_list, neighbours, embed, atom_ref,
           w_up, gammas, w_rad, w_mix, readout):
    vmem = pl.BlockSpec(memory_space=pltpu.VMEM)
    smem = pl.BlockSpec(memory_space=pltpu.SMEM)
    forces, parts = pl.pallas_call(
        body,
        name="potential",
        out_shape=(jax.ShapeDtypeStruct((3, SL), F32), jax.ShapeDtypeStruct((8, 128), F32)),
        in_specs=[vmem, vmem, smem, smem, vmem, vmem, vmem, smem, vmem, smem, vmem, vmem, vmem],
        out_specs=(vmem, vmem),
        scratch_shapes=[
            pltpu.VMEM((8, 2 * BLK), F32),
            pltpu.VMEM((2, 8, BLK), F32),
            pltpu.VMEM((2, 8, BLK), F32),
            pltpu.VMEM((8, SL), F32),
            pltpu.VMEM((4, 8, E), F32),
            pltpu.VMEM((2, 8, 128), F32),
            pltpu.VMEM((4, 8, 128), F32),
            pltpu.VMEM((8, C), F32),
            pltpu.VMEM((EXT, E), BF16),
            pltpu.VMEM((SL, NG), BF16),
            pltpu.VMEM((8, 8, E), F32),
            pltpu.VMEM((2, 3, C, E), F32),
            pltpu.VMEM((2, 3, C, E), F32),
            pltpu.VMEM((2, C, E), F32),
            pltpu.VMEM((C, E), F32),
            pltpu.VMEM((2, 8, C, SL), F32),
            pltpu.VMEM((C, SL), F32),
            pltpu.VMEM((C, SL), F32),
            pltpu.VMEM((NG, C), F32),
            pltpu.VMEM((NG, C), F32),
            pltpu.VMEM((NG, C), F32),
            pltpu.VMEM((NG, C), F32),
            pltpu.VMEM((2, 8, 128), F32),
            pltpu.VMEM((4, 8, 128), F32),
            pltpu.VMEM((9, 8, E), F32),
            pltpu.SemaphoreType.DMA((18,)),
            pltpu.SemaphoreType.DMA((18,)),
        ],
        compiler_params=pltpu.CompilerParams(collective_id=0, has_side_effects=True),
    )(old_pos, old_species, block_dest, block_count, send_list, neighbours, embed, atom_ref,
      w_up, gammas, w_rad, w_mix, readout)
    total, count = lax.psum((jnp.sum(parts[0]), jnp.sum(parts[1])), ("gx", "yz"))
    return forces, total / count


def solution(mesh):
    both = ("gx", "yz")
    return jax.shard_map(
        shards,
        mesh=mesh,
        in_specs=(
            P(None, both), P(both), P(both, None), P(both), P(both, None), P(None, both),
            P(), P(), P(), P(), P(), P(), P(),
        ),
        out_specs=(P(None, both), P()),
        check_vma=False,
    )
```

```python
import math

import jax
import jax.numpy as jnp
from jax import lax
from jax.experimental import pallas as pl
from jax.experimental.pallas import tpu as pltpu
from jax.sharding import PartitionSpec as P

MESH = pl.DeviceIdType.MESH
F32 = jnp.float32
BF16 = jnp.bfloat16

R3 = math.sqrt(3.0)
R15 = math.sqrt(15.0)
R5 = math.sqrt(5.0)
DEGREE = (0, 1, 1, 1, 2, 2, 2, 2, 2)

C = 128
NE = 4
BLK = 128
SL = 384
GH = 64
NG = 4 * GH
EXT = SL + NG
E = NE * SL
NN = (((1,), (0,)), ((), ()))
NT = (((1,), (1,)), ((), ()))
TN = (((0,), (0,)), ((), ()))


def dot(a, b, dims=NN):
    return lax.dot_general(a, b, dims, preferred_element_type=F32)


def head(x):
    return x.astype(BF16).astype(F32)


def parts2(x):
    hi = x.astype(BF16)
    return hi, (x - hi.astype(F32)).astype(BF16)


def stack3(x):
    hi = head(x)
    mid = head(x - hi)
    return jnp.concatenate([hi, mid, x - hi - mid], axis=0).astype(BF16)


def fold3(x):
    return x[0:8] + x[8:16] + x[16:24]


def weight_lhs(w):
    hi, lo = parts2(w)
    return jnp.concatenate([hi, hi, lo], axis=1)


def weight_dot(lhs, x, dims=NN):
    hi, lo = parts2(x)
    return dot(lhs, jnp.concatenate([hi, lo, hi], axis=0 if dims is NN else 1), dims)


def body(
    pos_in, species_in, dest_in, count_in, list_in, near_in, embed_in, atom_in, up_in, gamma_in,
    rad_in, mix_in, read_in,
    force_out, energy_out,
    tile_ref, mig_send, mig_recv, a_ref, tail_ref, gsend, grecv, emb_ref,
    oh_ref, soh_ref, y_ref, r_ref, rp_ref, p_ref, gp_ref, acc_ref, b_ref, gb_ref,
    psend, precv, bsend, brecv, fsend, frecv, gy_ref, plane, column, ring, send_sem, recv_sem,
):
    gx, yz = lax.axis_index("gx"), lax.axis_index("yz")
    n_gx, n_yz = lax.axis_size("gx"), lax.axis_size("yz")
    xp = (lax.rem(gx + 1, n_gx), yz)
    xm = (lax.rem(gx + n_gx - 1, n_gx), yz)
    yp = (gx, lax.rem(yz + 1, n_yz))
    ym = (gx, lax.rem(yz + n_yz - 1, n_yz))

    x_lo, z, core = yz // 32, lax.rem(yz // 2, 16), lax.rem(yz, 2)
    z_hi, z_lo = z // 4, lax.rem(z, 4)

    def place(xl, zh, zl, c):
        return xl * 32 + zh * 8 + zl * 2 + c

    plane_partners = [
        (lax.rem(gx + d, n_gx), place(lax.rem(x_lo + b, 2), z_hi, z_lo, core))
        for d in range(8) for b in range(2) if d or b
    ]
    column_partners = [
        (gx, place(x_lo, z_hi, lax.rem(z_lo + d, 4), lax.rem(core + b, 2)))
        for d in range(4) for b in range(2) if d or b
    ]
    ring_partners = [(gx, place(x_lo, lax.rem(z_hi + d, 4), z_lo, core)) for d in (1, 3)]

    barrier = pltpu.get_barrier_semaphore()
    greeted = [yp, ym] + plane_partners + column_partners + ring_partners
    for there in greeted:
        pl.semaphore_signal(barrier, inc=1, device_id=there, device_id_type=MESH)

    def copy(src, dst, number, there):
        return pltpu.make_async_remote_copy(
            src_ref=src, dst_ref=dst, send_sem=send_sem.at[number], recv_sem=recv_sem.at[number],
            device_id=there, device_id_type=MESH,
        )

    sub = lax.broadcasted_iota(jnp.int32, (8, 128), 0)
    lane = lax.broadcasted_iota(jnp.int32, (8, 128), 1)

    for b in range(2):
        kinds = jnp.broadcast_to(species_in[b * BLK:(b + 1) * BLK].reshape(1, BLK), (8, BLK))
        here = (kinds == sub - 3) & (lane < count_in[b])
        tile_ref[:, b * BLK:(b + 1) * BLK] = jnp.where(here, 1.0, 0.0).astype(F32)
    tile_ref[0:3, :] = pos_in[...]
    first, second = tile_ref[:, 0:BLK], tile_ref[:, BLK:2 * BLK]

    def packed(d):
        return jnp.where(dest_in[0, 0] == d, first, jnp.where(dest_in[0, 1] == d, second, 0.0))

    mig_send[0] = packed(0)
    mig_send[1] = packed(2)
    a_ref[:, BLK:2 * BLK] = packed(1)
    pl.semaphore_wait(barrier, len(greeted))
    moves = [copy(mig_send.at[0], mig_recv.at[0], 0, ym), copy(mig_send.at[1], mig_recv.at[1], 1, yp)]
    for move in moves:
        move.start()

    for pair in range(2):
        row = jnp.concatenate([list_in[2 * pair:2 * pair + 1, :], list_in[2 * pair + 1:2 * pair + 2, :]], axis=1)
        at = lax.broadcasted_iota(jnp.int32, (SL, 128), 0)
        soh_ref[:, pair * 128:(pair + 1) * 128] = jnp.where(at == row, 1.0, 0.0).astype(BF16)
    for k in range(NE):
        row = near_in[k:k + 1, :]

        def fill(block, _, row=row, k=k):
            base = pl.multiple_of(block * 128, 128)
            at = lax.broadcasted_iota(jnp.int32, (128, SL), 0) + base
            oh_ref[pl.ds(base, 128), k * SL:(k + 1) * SL] = jnp.where(at == row, 1.0, 0.0).astype(BF16)
            return 0

        lax.fori_loop(0, EXT // 128, fill, 0)

    emb_ref[...] = jnp.zeros((8, C), F32)
    emb_ref[3:8, :] = embed_in[...]
    emb24 = stack3(emb_ref[...])
    table24 = stack3(weight_dot(weight_lhs(emb_ref[...]), up_in[0]))
    mix_t = [weight_lhs(mix_in[t].T) for t in range(2)]
    mix_n = [weight_lhs(mix_in[t]) for t in range(2)]
    up1_t = weight_lhs(up_in[1].T)
    up1_n = weight_lhs(up_in[1])
    reads = jnp.concatenate([read_in[...], jnp.zeros((6, C), F32)], axis=0).T
    read_col = [jnp.broadcast_to(reads[:, t:t + 1], (C, SL)) for t in range(2)]
    rad24 = []
    for t in range(2):
        hi = head(rad_in[t])
        rad24.append(jnp.concatenate([hi, hi, rad_in[t] - hi], axis=0).astype(BF16))

    def upright(values):
        out = jnp.zeros((8, 128), F32)
        for q in range(len(values)):
            if values[q] is not None:
                out = jnp.where(sub == q, values[q], out)
        return out

    gamma_col = [upright([gamma_in[t, q] for q in range(8)]) for t in range(2)]
    atom_col = upright([None, None, None] + [atom_in[q] for q in range(5)])

    for move in moves:
        move.wait()
    a_ref[:, 0:BLK] = mig_recv[0]
    a_ref[:, 2 * BLK:3 * BLK] = mig_recv[1]

    atoms = a_ref[...]
    atoms24 = stack3(atoms)
    picked = fold3(dot(atoms24, soh_ref[...]))
    gsend[0] = picked[:, 0:128]
    gsend[1] = picked[:, 128:256]
    ghosts = [copy(gsend.at[f // 2], grecv.at[f], 2 + f, (xp, xm, yp, ym)[f]) for f in range(4)]
    for ghost in ghosts:
        ghost.start()

    row_of = lax.broadcasted_iota(jnp.int32, (8, SL), 0)
    marks = jnp.where(row_of >= 3, atoms, 0.0)
    live = jnp.sum(marks, axis=0, keepdims=True)
    marks24 = jnp.concatenate([marks, marks, marks], axis=0).astype(BF16)
    h0 = dot(emb24, marks24, TN)
    near_local = fold3(dot(atoms24, oh_ref[0:SL, :]))

    for ghost in ghosts:
        ghost.wait()
    low = lane < GH
    ghost8 = jnp.concatenate([jnp.where(low, grecv[0], grecv[1]), jnp.where(low, grecv[2], grecv[3])], axis=1)
    near = near_local + fold3(dot(stack3(ghost8), oh_ref[SL:EXT, :]))

    def spread(rows, d):
        return jnp.broadcast_to(rows[d:d + 1, :], (8, rows.shape[1]))

    def offsets():
        out = []
        for d in range(3):
            there = spread(atoms, d)
            out.append(spread(near, d) - jnp.concatenate([there] * NE, axis=1))
        return out

    rx, ry, rz = offsets()
    sq = rx * rx + ry * ry + rz * rz
    inv = lax.rsqrt(1.0 + sq)
    ux, uy, uz = rx * inv, ry * inv, rz * inv
    y_ref[0] = R3 * ux
    y_ref[1] = R3 * uy
    y_ref[2] = R3 * uz
    y_ref[3] = R15 * ux * uy
    y_ref[4] = R15 * uy * uz
    y_ref[5] = (0.5 * R5) * (2.0 * uz * uz - ux * ux - uy * uy)
    y_ref[6] = R15 * ux * uz
    y_ref[7] = (0.5 * R15) * (ux * ux - uy * uy)
    for d, value in enumerate((rx, ry, rz, sq)):
        tail_ref[d] = value

    def basis(t):
        cols = jnp.concatenate([gamma_col[t]] * (E // 128), axis=1)
        return cols, 0.25 * jnp.exp(-cols * tail_ref[3])

    def radial(t, values, out_ref):
        hi = head(values)
        rows = jnp.concatenate([hi, values - hi, hi], axis=0).astype(BF16)
        for l in range(3):
            out_ref[t, l] = dot(rad24[t][:, l * C:(l + 1) * C], rows, TN)

    cols0, basis0 = basis(0)
    radial(0, basis0, r_ref)
    near_marks = jnp.where(lax.broadcasted_iota(jnp.int32, (8, E), 0) >= 3, near, 0.0)
    p_ref[0] = dot(table24, jnp.concatenate([near_marks] * 3, axis=0).astype(BF16), TN)

    def forward(t):
        def step(cb, _):
            r = pl.ds(pl.multiple_of(cb * 8, 8), 8)
            for lt in range(3):
                acc = [None] * 9
                for k in range(NE):
                    e = pl.ds(k * SL + lt * 128, 128)
                    p = p_ref[t, r, e]
                    terms = [r_ref[t, l, r, e] * p for l in range(3)]
                    for m in range(9):
                        value = terms[DEGREE[m]]
                        if m:
                            value = value * y_ref[m - 1, :, e]
                        acc[m] = value if acc[m] is None else acc[m] + value
                i = pl.ds(lt * 128, 128)
                total = acc[0]
                for m in range(1, 9):
                    acc_ref[t, m - 1, r, i] = acc[m]
                    total = total + acc[m] * acc[m]
                b_ref[r, i] = total
            return 0

        lax.fori_loop(0, C // 8, step, 0)
        mixed = weight_dot(mix_t[t], b_ref[...])
        return mixed, 1.0 / (1.0 + jnp.exp(-mixed))

    mixed0, gate0 = forward(0)
    h1 = live * (h0 + mixed0 * gate0)
    slope0 = live * (gate0 * (1.0 + mixed0 * (1.0 - gate0)))

    p1 = weight_dot(up1_t, h1)
    p1_parts = jnp.concatenate(parts2(p1), axis=0)
    sent = dot(p1_parts, soh_ref[...])
    psend[...] = (sent[0:C] + sent[C:2 * C]).T
    faces = [pl.ds(f * GH, GH) for f in range(4)]
    outs = [copy(psend.at[faces[f]], precv.at[faces[f]], 6 + f, (xp, xm, yp, ym)[f]) for f in range(4)]
    for out in outs:
        out.start()

    cols1, basis1 = basis(1)
    radial(1, basis1, r_ref)
    radial(1, -cols1 * basis1, rp_ref)
    radial(0, -cols0 * basis0, rp_ref)
    local1 = dot(p1_parts, oh_ref[0:SL, :])
    p_ref[1] = local1[0:C] + local1[C:2 * C]

    for out in outs:
        out.wait()
    ghost1 = dot(jnp.concatenate(parts2(precv[...].T), axis=0), oh_ref[SL:EXT, :])
    p_ref[1] = p_ref[1] + (ghost1[0:C] + ghost1[C:2 * C])

    mixed1, gate1 = forward(1)
    h2 = live * (h1 + mixed1 * gate1)
    value = h1 * read_col[0] + h2 * read_col[1]
    rows = jnp.sum(value, axis=0, keepdims=True)
    cols3 = jnp.concatenate([atom_col] * 3, axis=1)
    rows = rows + jnp.sum(marks * cols3, axis=0, keepdims=True)
    row_e = rows[:, 0:128] + rows[:, 128:256] + rows[:, 256:384]
    row_n = live[:, 0:128] + live[:, 128:256] + live[:, 256:384]
    low1 = lax.broadcasted_iota(jnp.int32, (1, 128), 1) < 64
    row_e = row_e + pltpu.roll(row_e, 64, 1)
    row_n = row_n + pltpu.roll(row_n, 64, 1)
    mine = gx * 2 + x_lo
    plane[mine] = jnp.where(low1, row_e, row_n)
    shares = [copy(plane.at[mine], plane.at[mine], 18 + n, there) for n, there in enumerate(plane_partners)]
    for item in shares:
        item.start()

    def backward(t):
        for lt in range(3):
            i = pl.ds(lt * 128, 128)
            for pair in range(2):
                edges = [pl.ds((2 * pair + kk) * SL + lt * 128, 128) for kk in range(2)]

                def step(cb, carry, i=i, edges=edges):
                    r = pl.ds(pl.multiple_of(cb * 8, 8), 8)
                    carry = list(carry)
                    g0 = gb_ref[r, i]
                    g = [g0] + [acc_ref[t, m, r, i] * (g0 + g0) for m in range(8)]
                    for kk, e in enumerate(edges):
                        p = p_ref[t, r, e]
                        y = [y_ref[m, :, e] for m in range(8)]
                        s1 = g[1] * y[0] + g[2] * y[1] + g[3] * y[2]
                        s2 = g[4] * y[3] + g[5] * y[4] + g[6] * y[5] + g[7] * y[6] + g[8] * y[7]
                        radial1, radial2 = r_ref[t, 1, r, e], r_ref[t, 2, r, e]
                        if t:
                            gp_ref[r, e] = r_ref[t, 0, r, e] * g0 + radial1 * s1 + radial2 * s2
                        slope = rp_ref[t, 0, r, e] * g0 + rp_ref[t, 1, r, e] * s1 + rp_ref[t, 2, r, e] * s2
                        t1, t2 = radial1 * p, radial2 * p
                        at = kk * 9
                        for m in range(8):
                            carry[at + m] = carry[at + m] + g[m + 1] * (t1 if m < 3 else t2)
                        carry[at + 8] = carry[at + 8] + p * slope
                    return tuple(carry)

                if t:
                    init = tuple(jnp.zeros((8, 128), F32) for _ in range(18))
                else:
                    init = tuple(gy_ref[m, :, e] for e in edges for m in range(9))
                done = lax.fori_loop(0, C // 8, step, init)
                for kk, e in enumerate(edges):
                    for m in range(9):
                        gy_ref[m, :, e] = done[kk * 9 + m]

    slope1 = live * (gate1 * (1.0 + mixed1 * (1.0 - gate1)))
    gb_ref[...] = weight_dot(mix_n[1], slope1 * read_col[1])
    backward(1)

    gp_parts = jnp.concatenate(parts2(gp_ref[...]), axis=0)
    back = dot(oh_ref[SL:EXT, :], gp_parts, NT)
    bsend[...] = back[:, 0:C] + back[:, C:2 * C]
    returns = [copy(bsend.at[faces[f]], brecv.at[faces[f]], 10 + f, (xm, xp, ym, yp)[f]) for f in range(4)]
    for item in returns:
        item.start()
    stay = dot(oh_ref[0:SL, :], gp_parts, NT)
    g_p = stay[:, 0:C] + stay[:, C:2 * C]
    for item in shares:
        item.wait()
    mine = z_lo * 2 + core
    column[mine] = jnp.sum(plane[...], axis=0)
    shares = [copy(column.at[mine], column.at[mine], 33 + n, there) for n, there in enumerate(column_partners)]
    for item in shares:
        item.start()
    for item in returns:
        item.wait()
    came = dot(soh_ref[...], jnp.concatenate(parts2(brecv[...]), axis=1))
    g_p = g_p + (came[:, 0:C] + came[:, C:2 * C])
    g_h1 = weight_dot(up1_n, g_p, NT) + (read_col[0] + read_col[1])
    gb_ref[...] = weight_dot(mix_n[0], slope0 * g_h1)
    for item in shares:
        item.wait()
    ring[z_hi] = jnp.sum(column[...], axis=0)
    shares = [copy(ring.at[z_hi], ring.at[z_hi], 40 + n, there) for n, there in enumerate(ring_partners)]
    for item in shares:
        item.start()
    backward(0)

    def summed(m):
        return jnp.sum(gy_ref[m], axis=0, keepdims=True)

    g1, g2, g3, g4, g5, g6, g7, g8 = [summed(m) for m in range(8)]
    g_sq = summed(8)
    rx, ry, rz, sq = [tail_ref[d][0:1, :] for d in range(4)]
    inv = lax.rsqrt(1.0 + sq)
    ux, uy, uz = rx * inv, ry * inv, rz * inv
    gux = R3 * g1 + R15 * (uy * g4 + uz * g7 + ux * g8) - R5 * (ux * g6)
    guy = R3 * g2 + R15 * (ux * g4 + uz * g5 - uy * g8) - R5 * (uy * g6)
    guz = R3 * g3 + R15 * (uy * g5 + ux * g7) + (2.0 * R5) * (uz * g6)
    twice = 2.0 * g_sq - (gux * rx + guy * ry + guz * rz) * (inv * inv * inv)
    g_edge = [gux * inv + twice * rx, guy * inv + twice * ry, guz * inv + twice * rz]
    row8 = lax.broadcasted_iota(jnp.int32, (8, E), 0)
    edge8 = jnp.where(row8 == 0, g_edge[0], jnp.where(row8 == 1, g_edge[1], jnp.where(row8 == 2, g_edge[2], 0.0)))
    edge24 = stack3(edge8)
    away = fold3(dot(edge24, oh_ref[SL:EXT, :], NT))
    fsend[0] = away[:, 0:128]
    fsend[1] = away[:, 128:256]
    lasts = [copy(fsend.at[f // 2], frecv.at[f], 14 + f, (xm, xp, ym, yp)[f]) for f in range(4)]
    for item in lasts:
        item.start()
    own = fold3(dot(edge24, oh_ref[0:SL, :], NT))
    for k in range(NE):
        own = own - edge8[:, k * SL:(k + 1) * SL]
    for item in shares:
        item.wait()
    behind = lax.rem(z_hi + 3, 4)
    share = copy(ring.at[behind], ring.at[behind], 42, ring_partners[0])
    share.start()
    for item in lasts:
        item.wait()
    back8 = jnp.concatenate([jnp.where(low, frecv[0], frecv[1]), jnp.where(low, frecv[2], frecv[3])], axis=1)
    own = own + fold3(dot(stack3(back8), soh_ref[...], NT))
    force_out[...] = -own[0:3, :]
    share.wait()
    both = jnp.sum(ring[...], axis=0)
    total = jnp.sum(jnp.where(low1, both, 0.0), axis=1, keepdims=True)
    number = jnp.sum(jnp.where(low1, 0.0, both), axis=1, keepdims=True)
    energy_out[0] = jnp.sum(total / number)


def shards(old_pos, old_species, block_dest, block_count, send_list, neighbours, embed, atom_ref,
           w_up, gammas, w_rad, w_mix, readout):
    vmem = pl.BlockSpec(memory_space=pltpu.VMEM)
    smem = pl.BlockSpec(memory_space=pltpu.SMEM)
    forces, energy = pl.pallas_call(
        body,
        name="potential",
        out_shape=(jax.ShapeDtypeStruct((3, SL), F32), jax.ShapeDtypeStruct((1,), F32)),
        in_specs=[vmem, vmem, smem, smem, vmem, vmem, vmem, smem, vmem, smem, vmem, vmem, vmem],
        out_specs=(vmem, smem),
        scratch_shapes=[
            pltpu.VMEM((8, 2 * BLK), F32),
            pltpu.VMEM((2, 8, BLK), F32),
            pltpu.VMEM((2, 8, BLK), F32),
            pltpu.VMEM((8, SL), F32),
            pltpu.VMEM((4, 8, E), F32),
            pltpu.VMEM((2, 8, 128), F32),
            pltpu.VMEM((4, 8, 128), F32),
            pltpu.VMEM((8, C), F32),
            pltpu.VMEM((EXT, E), BF16),
            pltpu.VMEM((SL, NG), BF16),
            pltpu.VMEM((8, 8, E), F32),
            pltpu.VMEM((2, 3, C, E), F32),
            pltpu.VMEM((2, 3, C, E), F32),
            pltpu.VMEM((2, C, E), F32),
            pltpu.VMEM((C, E), F32),
            pltpu.VMEM((2, 8, C, SL), F32),
            pltpu.VMEM((C, SL), F32),
            pltpu.VMEM((C, SL), F32),
            pltpu.VMEM((NG, C), F32),
            pltpu.VMEM((NG, C), F32),
            pltpu.VMEM((NG, C), F32),
            pltpu.VMEM((NG, C), F32),
            pltpu.VMEM((2, 8, 128), F32),
            pltpu.VMEM((4, 8, 128), F32),
            pltpu.VMEM((9, 8, E), F32),
            pltpu.VMEM((16, 1, 128), F32),
            pltpu.VMEM((8, 1, 128), F32),
            pltpu.VMEM((4, 1, 128), F32),
            pltpu.SemaphoreType.DMA((43,)),
            pltpu.SemaphoreType.DMA((43,)),
        ],
        compiler_params=pltpu.CompilerParams(collective_id=0, has_side_effects=True),
    )(old_pos, old_species, block_dest.T, block_count, send_list, neighbours, embed, atom_ref,
      w_up, gammas, w_rad, w_mix, readout)
    return forces, energy.reshape(())


def solution(mesh):
    both = ("gx", "yz")
    return jax.shard_map(
        shards,
        mesh=mesh,
        in_specs=(
            P(None, both), P(both), P(both, None), P(both), P(both, None), P(None, both),
            P(), P(), P(), P(), P(), P(), P(),
        ),
        out_specs=(P(None, both), P()),
        check_vma=False,
    )
```

```python
import math

import jax
import jax.numpy as jnp
from jax import lax
from jax.experimental import pallas as pl
from jax.experimental.pallas import tpu as pltpu
from jax.sharding import PartitionSpec as P

MESH = pl.DeviceIdType.MESH
F32 = jnp.float32
BF16 = jnp.bfloat16

R3 = math.sqrt(3.0)
R15 = math.sqrt(15.0)
R5 = math.sqrt(5.0)
DEGREE = (0, 1, 1, 1, 2, 2, 2, 2, 2)

C = 128
NE = 4
BLK = 128
SL = 384
GH = 64
NG = 4 * GH
EXT = SL + NG
E = NE * SL
NN = (((1,), (0,)), ((), ()))
NT = (((1,), (1,)), ((), ()))
TN = (((0,), (0,)), ((), ()))


def dot(a, b, dims=NN):
    return lax.dot_general(a, b, dims, preferred_element_type=F32)


def head(x):
    return x.astype(BF16).astype(F32)


def parts2(x):
    hi = x.astype(BF16)
    return hi, (x - hi.astype(F32)).astype(BF16)


def stack3(x):
    hi = head(x)
    mid = head(x - hi)
    return jnp.concatenate([hi, mid, x - hi - mid], axis=0).astype(BF16)


def fold3(x):
    return x[0:8] + x[8:16] + x[16:24]


def weight_lhs(w):
    hi, lo = parts2(w)
    return jnp.concatenate([hi, hi, lo], axis=1)


def weight_dot(lhs, x, dims=NN):
    hi, lo = parts2(x)
    return dot(lhs, jnp.concatenate([hi, lo, hi], axis=0 if dims is NN else 1), dims)


def body(
    pos_hbm, species_hbm, dest_hbm, count_hbm, list_hbm, near_hbm, embed_hbm, atom_hbm, up_hbm, gamma_hbm,
    rad_hbm, mix_hbm, read_hbm,
    force_out, energy_out,
    pos_in, species_in, dest_in, count_in, list_in, near_in, embed_in, atom_in, up_in, gamma_in,
    rad_in, mix_in, read_in,
    tile_ref, mig_send, mig_recv, a_ref, tail_ref, gsend, grecv, emb_ref,
    oh_ref, soh_ref, y_ref, bs_ref, z_ref, r_ref, rp_ref, p_ref, gp_ref, acc0_ref, acc1_ref, b_ref, gb_ref, v_ref,
    psend, precv, bsend, brecv, fsend, frecv, gy_ref, plane, column, load_sem, know, send_sem, recv_sem,
):
    gx, yz = lax.axis_index("gx"), lax.axis_index("yz")
    n_gx, n_yz = lax.axis_size("gx"), lax.axis_size("yz")
    xp = (lax.rem(gx + 1, n_gx), yz)
    xm = (lax.rem(gx + n_gx - 1, n_gx), yz)
    yp = (gx, lax.rem(yz + 1, n_yz))
    ym = (gx, lax.rem(yz + n_yz - 1, n_yz))

    x_lo, z, core = yz // 32, lax.rem(yz // 2, 16), lax.rem(yz, 2)

    def along(dz, dc):
        return (gx, x_lo * 32 + lax.rem(z + dz + 16, 16) * 2 + lax.rem(core + dc, 2))

    plane_partners = [
        (lax.rem(gx + d, n_gx), lax.rem(x_lo + b, 2) * 32 + z * 2 + core)
        for d in (1, 7, 0, 2, 6, 3, 5, 4) for b in range(2) if d or b
    ]
    column_partners = [along(dz, dc) for dz in range(16) for dc in range(2) if dz or dc]
    relays = [along(4, 0), along(-4, 0)]

    barrier = pltpu.get_barrier_semaphore()
    greeted = [yp, ym] + plane_partners
    greeted += [along(dz, dc) for dz in (0, 1, -1, 2, -2, 3, -3, 4, -4) for dc in range(2) if dz or dc]

    def greet(those):
        for there in those:
            pl.semaphore_signal(barrier, inc=1, device_id=there, device_id_type=MESH)

    greet(greeted[0:4])
    loads = {}
    for n, (src, dst) in enumerate((
        (pos_hbm, pos_in), (species_hbm, species_in), (dest_hbm, dest_in), (count_hbm, count_in),
        (list_hbm, list_in), (near_hbm, near_in), (embed_hbm, embed_in), (up_hbm, up_in),
        (rad_hbm, rad_in), (gamma_hbm, gamma_in), (mix_hbm, mix_in), (read_hbm, read_in), (atom_hbm, atom_in),
    )):
        loads[n] = pltpu.make_async_copy(src, dst, load_sem.at[n])
        loads[n].start()
    greet(greeted[4:])

    def copy(src, dst, number, there):
        return pltpu.make_async_remote_copy(
            src_ref=src, dst_ref=dst, send_sem=send_sem.at[number], recv_sem=recv_sem.at[number],
            device_id=there, device_id_type=MESH,
        )

    sub = lax.broadcasted_iota(jnp.int32, (8, 128), 0)
    lane = lax.broadcasted_iota(jnp.int32, (8, 128), 1)

    for n in range(4):
        loads[n].wait()
    for b in range(2):
        kinds = jnp.broadcast_to(species_in[b * BLK:(b + 1) * BLK].reshape(1, BLK), (8, BLK))
        here = (kinds == sub - 3) & (lane < count_in[b])
        tile_ref[:, b * BLK:(b + 1) * BLK] = jnp.where(here, 1.0, 0.0).astype(F32)
    tile_ref[0:3, :] = pos_in[...]
    first, second = tile_ref[:, 0:BLK], tile_ref[:, BLK:2 * BLK]

    def packed(d):
        return jnp.where(dest_in[0, 0] == d, first, jnp.where(dest_in[0, 1] == d, second, 0.0))

    mig_send[0] = packed(0)
    mig_send[1] = packed(2)
    a_ref[:, BLK:2 * BLK] = packed(1)
    pl.semaphore_wait(barrier, len(greeted))
    moves = [copy(mig_send.at[0], mig_recv.at[0], 0, ym), copy(mig_send.at[1], mig_recv.at[1], 1, yp)]
    for move in moves:
        move.start()
    for there in relays:
        pl.semaphore_signal(know, inc=1, device_id=there, device_id_type=MESH)

    loads[4].wait()
    for pair in range(2):
        row = jnp.concatenate([list_in[2 * pair:2 * pair + 1, :], list_in[2 * pair + 1:2 * pair + 2, :]], axis=1)
        at = lax.broadcasted_iota(jnp.int32, (SL, 128), 0)
        soh_ref[:, pair * 128:(pair + 1) * 128] = jnp.where(at == row, 1.0, 0.0).astype(BF16)
    loads[5].wait()
    for k in range(NE):
        row = near_in[k:k + 1, :]

        def fill(block, _, row=row, k=k):
            base = pl.multiple_of(block * 128, 128)
            at = lax.broadcasted_iota(jnp.int32, (128, SL), 0) + base
            oh_ref[pl.ds(base, 128), k * SL:(k + 1) * SL] = jnp.where(at == row, 1.0, 0.0).astype(BF16)
            return 0

        lax.fori_loop(0, EXT // 128, fill, 0)

    for move in moves:
        move.wait()
    a_ref[:, 0:BLK] = mig_recv[0]
    a_ref[:, 2 * BLK:3 * BLK] = mig_recv[1]

    atoms = a_ref[...]
    atoms24 = stack3(atoms)
    picked = fold3(dot(atoms24, soh_ref[...]))
    gsend[0] = picked[:, 0:128]
    gsend[1] = picked[:, 128:256]
    ghosts = [copy(gsend.at[f // 2], grecv.at[f], 2 + f, (xp, xm, yp, ym)[f]) for f in range(4)]
    for ghost in ghosts:
        ghost.start()

    for n in range(6, 13):
        loads[n].wait()
    row_of = lax.broadcasted_iota(jnp.int32, (8, SL), 0)
    marks = jnp.where(row_of >= 3, atoms, 0.0)
    live = jnp.sum(marks, axis=0, keepdims=True)
    marks24 = jnp.concatenate([marks, marks, marks], axis=0).astype(BF16)
    near_local = fold3(dot(atoms24, oh_ref[0:SL, :]))

    emb_ref[...] = jnp.zeros((8, C), F32)
    emb_ref[3:8, :] = embed_in[...]
    h0 = dot(stack3(emb_ref[...]), marks24, TN)
    table = weight_dot(weight_lhs(emb_ref[...]), up_in[0])
    mix_t = [weight_lhs(mix_in[t].T) for t in range(2)]
    mix_n = [weight_lhs(mix_in[t]) for t in range(2)]
    up1_t = weight_lhs(up_in[1].T)
    up1_n = weight_lhs(up_in[1])
    reads = jnp.concatenate([read_in[...], jnp.zeros((6, C), F32)], axis=0).T
    read_col = [jnp.broadcast_to(reads[:, t:t + 1], (C, SL)) for t in range(2)]

    low_n, low_t = [], []
    for l in range(3):
        part = rad_in[0, :, l * C:(l + 1) * C]
        rows = jnp.concatenate([part * table[3 + q:4 + q, :] for q in range(5)], axis=0)
        hi = head(rows)
        low_n.append(weight_lhs(rows))
        low_t.append(jnp.concatenate([hi, hi, rows - hi, jnp.zeros((8, C), F32)], axis=0).T.astype(BF16))
    hi = head(rad_in[1])
    rad24 = jnp.concatenate([hi, hi, rad_in[1] - hi], axis=0).astype(BF16)

    def upright(values):
        out = jnp.zeros((8, 128), F32)
        for q in range(len(values)):
            if values[q] is not None:
                out = jnp.where(sub == q, values[q], out)
        return out

    gamma_col = [upright([gamma_in[t, q] for q in range(8)]) for t in range(2)]
    atom_col = upright([None, None, None] + [atom_in[q] for q in range(5)])

    for ghost in ghosts:
        ghost.wait()
    low = lane < GH
    ghost8 = jnp.concatenate([jnp.where(low, grecv[0], grecv[1]), jnp.where(low, grecv[2], grecv[3])], axis=1)
    near = near_local + fold3(dot(stack3(ghost8), oh_ref[SL:EXT, :]))

    def spread(rows, d):
        return jnp.broadcast_to(rows[d:d + 1, :], (8, rows.shape[1]))

    def offsets():
        out = []
        for d in range(3):
            there = spread(atoms, d)
            out.append(spread(near, d) - jnp.concatenate([there] * NE, axis=1))
        return out

    rx, ry, rz = offsets()
    sq = rx * rx + ry * ry + rz * rz
    inv = lax.rsqrt(1.0 + sq)
    ux, uy, uz = rx * inv, ry * inv, rz * inv
    y_ref[0] = R3 * ux
    y_ref[1] = R3 * uy
    y_ref[2] = R3 * uz
    y_ref[3] = R15 * ux * uy
    y_ref[4] = R15 * uy * uz
    y_ref[5] = (0.5 * R5) * (2.0 * uz * uz - ux * ux - uy * uy)
    y_ref[6] = R15 * ux * uz
    y_ref[7] = (0.5 * R15) * (ux * ux - uy * uy)
    for d, value in enumerate((rx, ry, rz, sq)):
        tail_ref[d] = value

    def basis(t):
        cols = jnp.concatenate([gamma_col[t]] * (E // 128), axis=1)
        return cols, 0.25 * jnp.exp(-cols * tail_ref[3])

    basis0 = basis(0)[1]
    for q in range(5):
        bs_ref[q] = basis0 * spread(near, 3 + q)

    for q in range(5):
        for lt in range(3):
            acc = [None] * 9
            for k in range(NE):
                e = pl.ds(k * SL + lt * 128, 128)
                b = bs_ref[q, :, e]
                for m in range(9):
                    value = b * y_ref[m - 1, :, e] if m else b
                    acc[m] = value if acc[m] is None else acc[m] + value
            for m in range(9):
                z_ref[q * 8:(q + 1) * 8, m * SL + lt * 128:m * SL + (lt + 1) * 128] = acc[m]

    total = None
    for m in range(9):
        block = z_ref[:, m * SL:(m + 1) * SL]
        hi = head(block)
        rows = jnp.concatenate([hi, block - hi, hi, jnp.zeros((8, SL), F32)], axis=0).astype(BF16)
        value = dot(low_t[DEGREE[m]], rows)
        if m:
            acc0_ref[m - 1] = value
        total = value * value + total if m else value
    mixed0 = weight_dot(mix_t[0], total)
    gate0 = 1.0 / (1.0 + jnp.exp(-mixed0))
    h1 = live * (h0 + mixed0 * gate0)

    p1 = weight_dot(up1_t, h1)
    p1_parts = jnp.concatenate(parts2(p1), axis=0)
    sent = dot(p1_parts, soh_ref[...])
    psend[...] = (sent[0:C] + sent[C:2 * C]).T
    faces = [pl.ds(f * GH, GH) for f in range(4)]
    outs = [copy(psend.at[faces[f]], precv.at[faces[f]], 6 + f, (xp, xm, yp, ym)[f]) for f in range(4)]
    for out in outs:
        out.start()

    slope0 = live * (gate0 * (1.0 + mixed0 * (1.0 - gate0)))

    def radial(values, out_ref):
        hi = head(values)
        rows = jnp.concatenate([hi, values - hi, hi], axis=0).astype(BF16)
        for l in range(3):
            out_ref[l] = dot(rad24[:, l * C:(l + 1) * C], rows, TN)

    cols1, basis1 = basis(1)
    radial(basis1, r_ref)
    radial(-cols1 * basis1, rp_ref)
    local1 = dot(p1_parts, oh_ref[0:SL, :])
    p_ref[...] = local1[0:C] + local1[C:2 * C]

    for out in outs:
        out.wait()
    ghost1 = dot(jnp.concatenate(parts2(precv[...].T), axis=0), oh_ref[SL:EXT, :])
    p_ref[...] = p_ref[...] + (ghost1[0:C] + ghost1[C:2 * C])

    def forward(cb, _):
        r = pl.ds(pl.multiple_of(cb * 8, 8), 8)
        for lt in range(3):
            acc = [None] * 9
            for k in range(NE):
                e = pl.ds(k * SL + lt * 128, 128)
                p = p_ref[r, e]
                terms = [r_ref[l, r, e] * p for l in range(3)]
                for m in range(9):
                    value = terms[DEGREE[m]]
                    if m:
                        value = value * y_ref[m - 1, :, e]
                    acc[m] = value if acc[m] is None else acc[m] + value
            i = pl.ds(lt * 128, 128)
            total = acc[0]
            for m in range(1, 9):
                acc1_ref[m - 1, r, i] = acc[m]
                total = total + acc[m] * acc[m]
            b_ref[r, i] = total
        return 0

    lax.fori_loop(0, C // 8, forward, 0)
    mixed1 = weight_dot(mix_t[1], b_ref[...])
    gate1 = 1.0 / (1.0 + jnp.exp(-mixed1))
    h2 = live * (h1 + mixed1 * gate1)
    value = h1 * read_col[0] + h2 * read_col[1]
    rows = jnp.sum(value, axis=0, keepdims=True)
    cols3 = jnp.concatenate([atom_col] * 3, axis=1)
    rows = rows + jnp.sum(marks * cols3, axis=0, keepdims=True)
    row_e = rows[:, 0:128] + rows[:, 128:256] + rows[:, 256:384]
    row_n = live[:, 0:128] + live[:, 128:256] + live[:, 256:384]
    low1 = lax.broadcasted_iota(jnp.int32, (1, 128), 1) < 64
    row_e = row_e + pltpu.roll(row_e, 64, 1)
    row_n = row_n + pltpu.roll(row_n, 64, 1)
    mine = gx * 2 + x_lo
    plane[mine] = jnp.where(low1, row_e, row_n)
    shares = [copy(plane.at[mine], plane.at[mine], 18 + n, there) for n, there in enumerate(plane_partners)]
    for item in shares:
        item.start()

    slope1 = live * (gate1 * (1.0 + mixed1 * (1.0 - gate1)))
    gb_ref[...] = weight_dot(mix_n[1], slope1 * read_col[1])
    for lt in range(3):
        i = pl.ds(lt * 128, 128)
        for pair in range(2):
            edges = [pl.ds((2 * pair + kk) * SL + lt * 128, 128) for kk in range(2)]

            def step(cb, carry, i=i, edges=edges):
                r = pl.ds(pl.multiple_of(cb * 8, 8), 8)
                carry = list(carry)
                g0 = gb_ref[r, i]
                g = [g0] + [acc1_ref[m, r, i] * (g0 + g0) for m in range(8)]
                for kk, e in enumerate(edges):
                    p = p_ref[r, e]
                    y = [y_ref[m, :, e] for m in range(8)]
                    s1 = g[1] * y[0] + g[2] * y[1] + g[3] * y[2]
                    s2 = g[4] * y[3] + g[5] * y[4] + g[6] * y[5] + g[7] * y[6] + g[8] * y[7]
                    radial1, radial2 = r_ref[1, r, e], r_ref[2, r, e]
                    gp_ref[r, e] = r_ref[0, r, e] * g0 + radial1 * s1 + radial2 * s2
                    slope = rp_ref[0, r, e] * g0 + rp_ref[1, r, e] * s1 + rp_ref[2, r, e] * s2
                    t1, t2 = radial1 * p, radial2 * p
                    at = kk * 9
                    for m in range(8):
                        carry[at + m] = carry[at + m] + g[m + 1] * (t1 if m < 3 else t2)
                    carry[at + 8] = carry[at + 8] + p * slope
                return tuple(carry)

            done = lax.fori_loop(0, C // 8, step, tuple(jnp.zeros((8, 128), F32) for _ in range(18)))
            for kk, e in enumerate(edges):
                for m in range(9):
                    gy_ref[m, :, e] = done[kk * 9 + m]

    gp_parts = jnp.concatenate(parts2(gp_ref[...]), axis=0)
    back = dot(oh_ref[SL:EXT, :], gp_parts, NT)
    bsend[...] = back[:, 0:C] + back[:, C:2 * C]
    returns = [copy(bsend.at[faces[f]], brecv.at[faces[f]], 10 + f, (xm, xp, ym, yp)[f]) for f in range(4)]
    for item in returns:
        item.start()
    stay = dot(oh_ref[0:SL, :], gp_parts, NT)
    g_p = stay[:, 0:C] + stay[:, C:2 * C]
    pl.semaphore_wait(know, 2)
    for item in shares:
        item.wait()
    mine = z * 2 + core
    column[mine] = jnp.sum(plane[...], axis=0)
    shares = [copy(column.at[mine], column.at[mine], 33 + n, there) for n, there in enumerate(column_partners)]
    for item in shares:
        item.start()
    for item in returns:
        item.wait()
    came = dot(soh_ref[...], jnp.concatenate(parts2(brecv[...]), axis=1))
    g_p = g_p + (came[:, 0:C] + came[:, C:2 * C])
    g_h1 = weight_dot(up1_n, g_p, NT) + (read_col[0] + read_col[1])
    g_b = weight_dot(mix_n[0], slope0 * g_h1)

    for m in range(9):
        g = acc0_ref[m - 1] * (g_b + g_b) if m else g_b
        v_ref[m] = weight_dot(low_n[DEGREE[m]], g)
    for lt in range(3):
        i = pl.ds(lt * 128, 128)
        for k in range(NE):
            e = pl.ds(k * SL + lt * 128, 128)
            y = [y_ref[m, :, e] for m in range(8)]
            sums = [gy_ref[m, :, e] for m in range(8)]
            slope = None
            for q in range(5):
                b = bs_ref[q, :, e]
                mixed = v_ref[0, q * 8:(q + 1) * 8, i]
                for m in range(8):
                    v = v_ref[m + 1, q * 8:(q + 1) * 8, i]
                    sums[m] = sums[m] + b * v
                    mixed = mixed + y[m] * v
                slope = b * mixed if slope is None else slope + b * mixed
            for m in range(8):
                gy_ref[m, :, e] = sums[m]
            gy_ref[8, :, e] = gy_ref[8, :, e] - gamma_col[0] * slope

    def summed(m):
        return jnp.sum(gy_ref[m], axis=0, keepdims=True)

    g1, g2, g3, g4, g5, g6, g7, g8 = [summed(m) for m in range(8)]
    g_sq = summed(8)
    rx, ry, rz, sq = [tail_ref[d][0:1, :] for d in range(4)]
    inv = lax.rsqrt(1.0 + sq)
    ux, uy, uz = rx * inv, ry * inv, rz * inv
    gux = R3 * g1 + R15 * (uy * g4 + uz * g7 + ux * g8) - R5 * (ux * g6)
    guy = R3 * g2 + R15 * (ux * g4 + uz * g5 - uy * g8) - R5 * (uy * g6)
    guz = R3 * g3 + R15 * (uy * g5 + ux * g7) + (2.0 * R5) * (uz * g6)
    twice = 2.0 * g_sq - (gux * rx + guy * ry + guz * rz) * (inv * inv * inv)
    g_edge = [gux * inv + twice * rx, guy * inv + twice * ry, guz * inv + twice * rz]
    row8 = lax.broadcasted_iota(jnp.int32, (8, E), 0)
    edge8 = jnp.where(row8 == 0, g_edge[0], jnp.where(row8 == 1, g_edge[1], jnp.where(row8 == 2, g_edge[2], 0.0)))
    edge24 = stack3(edge8)
    away = fold3(dot(edge24, oh_ref[SL:EXT, :], NT))
    fsend[0] = away[:, 0:128]
    fsend[1] = away[:, 128:256]
    lasts = [copy(fsend.at[f // 2], frecv.at[f], 14 + f, (xm, xp, ym, yp)[f]) for f in range(4)]
    for item in lasts:
        item.start()
    own = fold3(dot(edge24, oh_ref[0:SL, :], NT))
    for k in range(NE):
        own = own - edge8[:, k * SL:(k + 1) * SL]
    for item in lasts:
        item.wait()
    back8 = jnp.concatenate([jnp.where(low, frecv[0], frecv[1]), jnp.where(low, frecv[2], frecv[3])], axis=1)
    own = own + fold3(dot(stack3(back8), soh_ref[...], NT))
    force_out[...] = -own[0:3, :]
    for item in shares:
        item.wait()
    both = jnp.sum(column[...], axis=0)
    total = jnp.sum(jnp.where(low1, both, 0.0), axis=1, keepdims=True)
    number = jnp.sum(jnp.where(low1, 0.0, both), axis=1, keepdims=True)
    energy_out[0] = jnp.sum(total / number)


def shards(old_pos, old_species, block_dest, block_count, send_list, neighbours, embed, atom_ref,
           w_up, gammas, w_rad, w_mix, readout):
    vmem = pl.BlockSpec(memory_space=pltpu.VMEM)
    smem = pl.BlockSpec(memory_space=pltpu.SMEM)
    forces, energy = pl.pallas_call(
        body,
        name="potential",
        out_shape=(jax.ShapeDtypeStruct((3, SL), F32), jax.ShapeDtypeStruct((1,), F32)),
        in_specs=[pl.BlockSpec(memory_space=pltpu.HBM)] * 13,
        out_specs=(vmem, smem),
        scratch_shapes=[
            pltpu.VMEM((3, 2 * BLK), F32),
            pltpu.VMEM((2 * BLK,), jnp.int32),
            pltpu.SMEM((1, 2), jnp.int32),
            pltpu.SMEM((2,), jnp.int32),
            pltpu.VMEM((4, GH), jnp.int32),
            pltpu.VMEM((NE, SL), jnp.int32),
            pltpu.VMEM((5, C), F32),
            pltpu.SMEM((5,), F32),
            pltpu.VMEM((2, C, C), F32),
            pltpu.SMEM((2, 8), F32),
            pltpu.VMEM((2, 8, 3 * C), F32),
            pltpu.VMEM((2, C, C), F32),
            pltpu.VMEM((2, C), F32),
            pltpu.VMEM((8, 2 * BLK), F32),
            pltpu.VMEM((2, 8, BLK), F32),
            pltpu.VMEM((2, 8, BLK), F32),
            pltpu.VMEM((8, SL), F32),
            pltpu.VMEM((4, 8, E), F32),
            pltpu.VMEM((2, 8, 128), F32),
            pltpu.VMEM((4, 8, 128), F32),
            pltpu.VMEM((8, C), F32),
            pltpu.VMEM((EXT, E), BF16),
            pltpu.VMEM((SL, NG), BF16),
            pltpu.VMEM((8, 8, E), F32),
            pltpu.VMEM((5, 8, E), F32),
            pltpu.VMEM((40, 9 * SL), F32),
            pltpu.VMEM((3, C, E), F32),
            pltpu.VMEM((3, C, E), F32),
            pltpu.VMEM((C, E), F32),
            pltpu.VMEM((C, E), F32),
            pltpu.VMEM((8, C, SL), F32),
            pltpu.VMEM((8, C, SL), F32),
            pltpu.VMEM((C, SL), F32),
            pltpu.VMEM((C, SL), F32),
            pltpu.VMEM((9, 40, SL), F32),
            pltpu.VMEM((NG, C), F32),
            pltpu.VMEM((NG, C), F32),
            pltpu.VMEM((NG, C), F32),
            pltpu.VMEM((NG, C), F32),
            pltpu.VMEM((2, 8, 128), F32),
            pltpu.VMEM((4, 8, 128), F32),
            pltpu.VMEM((9, 8, E), F32),
            pltpu.VMEM((16, 1, 128), F32),
            pltpu.VMEM((32, 1, 128), F32),
            pltpu.SemaphoreType.DMA((13,)),
            pltpu.SemaphoreType.REGULAR,
            pltpu.SemaphoreType.DMA((64,)),
            pltpu.SemaphoreType.DMA((64,)),
        ],
        compiler_params=pltpu.CompilerParams(collective_id=0, has_side_effects=True),
    )(old_pos, old_species, block_dest.T, block_count, send_list, neighbours, embed, atom_ref,
      w_up, gammas, w_rad, w_mix, readout)
    return forces, energy.reshape(())


def solution(mesh):
    both = ("gx", "yz")
    return jax.shard_map(
        shards,
        mesh=mesh,
        in_specs=(
            P(None, both), P(both), P(both, None), P(both), P(both, None), P(None, both),
            P(), P(), P(), P(), P(), P(), P(),
        ),
        out_specs=(P(None, both), P()),
        check_vma=False,
    )
```

```python
import math

import jax
import jax.numpy as jnp
from jax import lax
from jax.experimental import pallas as pl
from jax.experimental.pallas import tpu as pltpu
from jax.sharding import PartitionSpec as P

MESH = pl.DeviceIdType.MESH
F32 = jnp.float32
BF16 = jnp.bfloat16

R3 = math.sqrt(3.0)
R15 = math.sqrt(15.0)
R5 = math.sqrt(5.0)
DEGREE = (0, 1, 1, 1, 2, 2, 2, 2, 2)

C = 128
NE = 4
BLK = 128
SL = 384
GH = 64
NG = 4 * GH
EXT = SL + NG
E = NE * SL
NN = (((1,), (0,)), ((), ()))
NT = (((1,), (1,)), ((), ()))
TN = (((0,), (0,)), ((), ()))


def dot(a, b, dims=NN):
    return lax.dot_general(a, b, dims, preferred_element_type=F32)


def head(x):
    return x.astype(BF16).astype(F32)


def parts2(x):
    hi = x.astype(BF16)
    return hi, (x - hi.astype(F32)).astype(BF16)


def stack3(x):
    hi = head(x)
    mid = head(x - hi)
    return jnp.concatenate([hi, mid, x - hi - mid], axis=0).astype(BF16)


def fold3(x):
    return x[0:8] + x[8:16] + x[16:24]


def weight_lhs(w):
    hi, lo = parts2(w)
    return jnp.concatenate([hi, hi, lo], axis=1)


def weight_dot(lhs, x, dims=NN):
    hi, lo = parts2(x)
    return dot(lhs, jnp.concatenate([hi, lo, hi], axis=0 if dims is NN else 1), dims)


def body(
    pos_hbm, species_hbm, dest_hbm, count_hbm, list_hbm, near_hbm, embed_hbm, atom_hbm, up_hbm, gamma_hbm,
    rad_hbm, mix_hbm, read_hbm,
    force_out, energy_out,
    pos_in, species_in, dest_in, count_in, list_in, near_in, embed_in, atom_in, up_in, gamma_in,
    rad_in, mix_in, read_in,
    tile_ref, mig_send, mig_recv, a_ref, tail_ref, gsend, grecv, emb_ref,
    oh_ref, soh_ref, y_ref, bs_ref, z_ref, r_ref, rp_ref, p_ref, gp_ref, acc0_ref, acc1_ref, b_ref, gb_ref, v_ref, s_ref,
    psend, precv, bsend, brecv, fsend, frecv, gy_ref, plane, column, load_sem, know, send_sem, recv_sem,
):
    gx, yz = lax.axis_index("gx"), lax.axis_index("yz")
    n_gx, n_yz = lax.axis_size("gx"), lax.axis_size("yz")
    xp = (lax.rem(gx + 1, n_gx), yz)
    xm = (lax.rem(gx + n_gx - 1, n_gx), yz)
    yp = (gx, lax.rem(yz + 1, n_yz))
    ym = (gx, lax.rem(yz + n_yz - 1, n_yz))

    x_lo, z, core = yz // 32, lax.rem(yz // 2, 16), lax.rem(yz, 2)

    def along(dz, dc):
        return (gx, x_lo * 32 + lax.rem(z + dz + 16, 16) * 2 + lax.rem(core + dc, 2))

    plane_partners = [
        (lax.rem(gx + d, n_gx), lax.rem(x_lo + b, 2) * 32 + z * 2 + core)
        for d in (1, 7, 0, 2, 6, 3, 5, 4) for b in range(2) if d or b
    ]
    column_partners = [along(dz, dc) for dz in range(16) for dc in range(2) if dz or dc]
    relays = [along(4, 0), along(-4, 0)]

    barrier = pltpu.get_barrier_semaphore()
    greeted = [yp, ym] + plane_partners
    greeted += [along(dz, dc) for dz in (0, 1, -1, 2, -2, 3, -3, 4, -4) for dc in range(2) if dz or dc]

    def greet(those):
        for there in those:
            pl.semaphore_signal(barrier, inc=1, device_id=there, device_id_type=MESH)

    greet(greeted[0:4])
    loads = {}
    for n, (src, dst) in enumerate((
        (pos_hbm, pos_in), (species_hbm, species_in), (dest_hbm, dest_in), (count_hbm, count_in),
        (list_hbm, list_in), (near_hbm, near_in), (embed_hbm, embed_in), (up_hbm, up_in),
        (rad_hbm, rad_in), (gamma_hbm, gamma_in), (mix_hbm, mix_in), (read_hbm, read_in), (atom_hbm, atom_in),
    )):
        loads[n] = pltpu.make_async_copy(src, dst, load_sem.at[n])
        loads[n].start()
    greet(greeted[4:])

    def copy(src, dst, number, there):
        return pltpu.make_async_remote_copy(
            src_ref=src, dst_ref=dst, send_sem=send_sem.at[number], recv_sem=recv_sem.at[number],
            device_id=there, device_id_type=MESH,
        )

    sub = lax.broadcasted_iota(jnp.int32, (8, 128), 0)
    lane = lax.broadcasted_iota(jnp.int32, (8, 128), 1)

    for n in range(4):
        loads[n].wait()
    for b in range(2):
        kinds = jnp.broadcast_to(species_in[b * BLK:(b + 1) * BLK].reshape(1, BLK), (8, BLK))
        here = (kinds == sub - 3) & (lane < count_in[b])
        tile_ref[:, b * BLK:(b + 1) * BLK] = jnp.where(here, 1.0, 0.0).astype(F32)
    tile_ref[0:3, :] = pos_in[...]
    first, second = tile_ref[:, 0:BLK], tile_ref[:, BLK:2 * BLK]

    def packed(d):
        return jnp.where(dest_in[0, 0] == d, first, jnp.where(dest_in[0, 1] == d, second, 0.0))

    mig_send[0] = packed(0)
    mig_send[1] = packed(2)
    a_ref[:, BLK:2 * BLK] = packed(1)
    pl.semaphore_wait(barrier, len(greeted))
    moves = [copy(mig_send.at[0], mig_recv.at[0], 0, ym), copy(mig_send.at[1], mig_recv.at[1], 1, yp)]
    for move in moves:
        move.start()
    for there in relays:
        pl.semaphore_signal(know, inc=1, device_id=there, device_id_type=MESH)

    loads[4].wait()
    for pair in range(2):
        row = jnp.concatenate([list_in[2 * pair:2 * pair + 1, :], list_in[2 * pair + 1:2 * pair + 2, :]], axis=1)
        at = lax.broadcasted_iota(jnp.int32, (SL, 128), 0)
        soh_ref[:, pair * 128:(pair + 1) * 128] = jnp.where(at == row, 1.0, 0.0).astype(BF16)
    loads[5].wait()
    for k in range(NE):
        row = near_in[k:k + 1, :]

        def fill(block, _, row=row, k=k):
            base = pl.multiple_of(block * 128, 128)
            at = lax.broadcasted_iota(jnp.int32, (128, SL), 0) + base
            oh_ref[pl.ds(base, 128), k * SL:(k + 1) * SL] = jnp.where(at == row, 1.0, 0.0).astype(BF16)
            return 0

        lax.fori_loop(0, EXT // 128, fill, 0)

    for move in moves:
        move.wait()
    a_ref[:, 0:BLK] = mig_recv[0]
    a_ref[:, 2 * BLK:3 * BLK] = mig_recv[1]

    atoms = a_ref[...]
    atoms24 = stack3(atoms)
    picked = fold3(dot(atoms24, soh_ref[...]))
    gsend[0] = picked[:, 0:128]
    gsend[1] = picked[:, 128:256]
    ghosts = [copy(gsend.at[f // 2], grecv.at[f], 2 + f, (xp, xm, yp, ym)[f]) for f in range(4)]
    for ghost in ghosts:
        ghost.start()

    for n in range(6, 13):
        loads[n].wait()
    row_of = lax.broadcasted_iota(jnp.int32, (8, SL), 0)
    marks = jnp.where(row_of >= 3, atoms, 0.0)
    live = jnp.sum(marks, axis=0, keepdims=True)
    marks24 = jnp.concatenate([marks, marks, marks], axis=0).astype(BF16)
    near_local = fold3(dot(atoms24, oh_ref[0:SL, :]))

    emb_ref[...] = jnp.zeros((8, C), F32)
    emb_ref[3:8, :] = embed_in[...]
    h0 = dot(stack3(emb_ref[...]), marks24, TN)
    table = weight_dot(weight_lhs(emb_ref[...]), up_in[0])
    mix_t = [weight_lhs(mix_in[t].T) for t in range(2)]
    mix_n = [weight_lhs(mix_in[t]) for t in range(2)]
    up1_t = weight_lhs(up_in[1].T)
    up1_n = weight_lhs(up_in[1])
    reads = jnp.concatenate([read_in[...], jnp.zeros((6, C), F32)], axis=0).T
    read_col = [jnp.broadcast_to(reads[:, t:t + 1], (C, SL)) for t in range(2)]

    low_n, low_t = [], []
    for l in range(3):
        part = rad_in[0, :, l * C:(l + 1) * C]
        rows = jnp.concatenate([part * table[3 + q:4 + q, :] for q in range(5)], axis=0)
        hi = head(rows)
        low_n.append(weight_lhs(rows))
        low_t.append(jnp.concatenate([hi, hi, rows - hi, jnp.zeros((8, C), F32)], axis=0).T.astype(BF16))
    hi = head(rad_in[1])
    rad24 = jnp.concatenate([hi, hi, rad_in[1] - hi], axis=0).astype(BF16)

    def upright(values):
        out = jnp.zeros((8, 128), F32)
        for q in range(len(values)):
            if values[q] is not None:
                out = jnp.where(sub == q, values[q], out)
        return out

    gamma_col = [upright([gamma_in[t, q] for q in range(8)]) for t in range(2)]
    atom_col = upright([None, None, None] + [atom_in[q] for q in range(5)])

    for ghost in ghosts:
        ghost.wait()
    low = lane < GH
    ghost8 = jnp.concatenate([jnp.where(low, grecv[0], grecv[1]), jnp.where(low, grecv[2], grecv[3])], axis=1)
    near = near_local + fold3(dot(stack3(ghost8), oh_ref[SL:EXT, :]))

    def spread(rows, d):
        return jnp.broadcast_to(rows[d:d + 1, :], (8, rows.shape[1]))

    def offsets():
        out = []
        for d in range(3):
            there = spread(atoms, d)
            out.append(spread(near, d) - jnp.concatenate([there] * NE, axis=1))
        return out

    rx, ry, rz = offsets()
    sq = rx * rx + ry * ry + rz * rz
    inv = lax.rsqrt(1.0 + sq)
    ux, uy, uz = rx * inv, ry * inv, rz * inv
    y_ref[0] = R3 * ux
    y_ref[1] = R3 * uy
    y_ref[2] = R3 * uz
    y_ref[3] = R15 * ux * uy
    y_ref[4] = R15 * uy * uz
    y_ref[5] = (0.5 * R5) * (2.0 * uz * uz - ux * ux - uy * uy)
    y_ref[6] = R15 * ux * uz
    y_ref[7] = (0.5 * R15) * (ux * ux - uy * uy)
    for d, value in enumerate((rx, ry, rz, sq)):
        tail_ref[d] = value

    def basis(t):
        cols = jnp.concatenate([gamma_col[t]] * (E // 128), axis=1)
        return cols, 0.25 * jnp.exp(-cols * tail_ref[3])

    basis0 = basis(0)[1]
    for q in range(5):
        bs_ref[q] = basis0 * spread(near, 3 + q)

    for q in range(5):
        for lt in range(3):
            acc = [None] * 9
            for k in range(NE):
                e = pl.ds(k * SL + lt * 128, 128)
                b = bs_ref[q, :, e]
                for m in range(9):
                    value = b * y_ref[m - 1, :, e] if m else b
                    acc[m] = value if acc[m] is None else acc[m] + value
            for m in range(9):
                z_ref[q * 8:(q + 1) * 8, m * SL + lt * 128:m * SL + (lt + 1) * 128] = acc[m]

    total = None
    for m in range(9):
        block = z_ref[:, m * SL:(m + 1) * SL]
        hi = head(block)
        rows = jnp.concatenate([hi, block - hi, hi, jnp.zeros((8, SL), F32)], axis=0).astype(BF16)
        value = dot(low_t[DEGREE[m]], rows)
        if m:
            acc0_ref[m - 1] = value
        total = value * value + total if m else value
    mixed0 = weight_dot(mix_t[0], total)
    gate0 = 1.0 / (1.0 + jnp.exp(-mixed0))
    h1 = live * (h0 + mixed0 * gate0)

    p1 = weight_dot(up1_t, h1)
    p1_parts = jnp.concatenate(parts2(p1), axis=0)
    sent = dot(p1_parts, soh_ref[...])
    psend[...] = (sent[0:C] + sent[C:2 * C]).T
    faces = [pl.ds(f * GH, GH) for f in range(4)]
    outs = [copy(psend.at[faces[f]], precv.at[faces[f]], 6 + f, (xp, xm, yp, ym)[f]) for f in range(4)]
    for out in outs:
        out.start()

    slope0 = live * (gate0 * (1.0 + mixed0 * (1.0 - gate0)))

    def radial(values, out_ref):
        hi = head(values)
        rows = jnp.concatenate([hi, values - hi, hi], axis=0).astype(BF16)
        for l in range(3):
            out_ref[l] = dot(rad24[:, l * C:(l + 1) * C], rows, TN)

    cols1, basis1 = basis(1)
    radial(basis1, r_ref)
    radial(-cols1 * basis1, rp_ref)
    local1 = dot(p1_parts, oh_ref[0:SL, :])
    p_ref[...] = local1[0:C] + local1[C:2 * C]

    for out in outs:
        out.wait()
    ghost1 = dot(jnp.concatenate(parts2(precv[...].T), axis=0), oh_ref[SL:EXT, :])
    p_ref[...] = p_ref[...] + (ghost1[0:C] + ghost1[C:2 * C])

    def forward(cb, _):
        r = pl.ds(pl.multiple_of(cb * 8, 8), 8)
        for lt in range(3):
            acc = [None] * 9
            for k in range(NE):
                e = pl.ds(k * SL + lt * 128, 128)
                p = p_ref[r, e]
                terms = [r_ref[l, r, e] * p for l in range(3)]
                for m in range(9):
                    value = terms[DEGREE[m]]
                    if m:
                        value = value * y_ref[m - 1, :, e]
                    acc[m] = value if acc[m] is None else acc[m] + value
            i = pl.ds(lt * 128, 128)
            total = acc[0]
            for m in range(1, 9):
                acc1_ref[m - 1, r, i] = acc[m]
                total = total + acc[m] * acc[m]
            b_ref[r, i] = total
        return 0

    lax.fori_loop(0, C // 8, forward, 0)
    mixed1 = weight_dot(mix_t[1], b_ref[...])
    gate1 = 1.0 / (1.0 + jnp.exp(-mixed1))
    h2 = live * (h1 + mixed1 * gate1)
    value = h1 * read_col[0] + h2 * read_col[1]
    rows = jnp.sum(value, axis=0, keepdims=True)
    cols3 = jnp.concatenate([atom_col] * 3, axis=1)
    rows = rows + jnp.sum(marks * cols3, axis=0, keepdims=True)
    row_e = rows[:, 0:128] + rows[:, 128:256] + rows[:, 256:384]
    row_n = live[:, 0:128] + live[:, 128:256] + live[:, 256:384]
    low1 = lax.broadcasted_iota(jnp.int32, (1, 128), 1) < 64
    row_e = row_e + pltpu.roll(row_e, 64, 1)
    row_n = row_n + pltpu.roll(row_n, 64, 1)
    mine = gx * 2 + x_lo
    plane[mine] = jnp.where(low1, row_e, row_n)
    shares = [copy(plane.at[mine], plane.at[mine], 18 + n, there) for n, there in enumerate(plane_partners)]
    for item in shares:
        item.start()

    slope1 = live * (gate1 * (1.0 + mixed1 * (1.0 - gate1)))
    gb_ref[...] = weight_dot(mix_n[1], slope1 * read_col[1])
    def first_half(cb, _):
        r = pl.ds(pl.multiple_of(cb * 8, 8), 8)
        for lt in range(3):
            i = pl.ds(lt * 128, 128)
            g0 = gb_ref[r, i]
            g = [g0] + [acc1_ref[m, r, i] * (g0 + g0) for m in range(8)]
            for k in range(NE):
                e = pl.ds(k * SL + lt * 128, 128)
                y = [y_ref[m, :, e] for m in range(8)]
                s1 = g[1] * y[0] + g[2] * y[1] + g[3] * y[2]
                s2 = g[4] * y[3] + g[5] * y[4] + g[6] * y[5] + g[7] * y[6] + g[8] * y[7]
                s_ref[0, r, e] = s1
                s_ref[1, r, e] = s2
                gp_ref[r, e] = r_ref[0, r, e] * g0 + r_ref[1, r, e] * s1 + r_ref[2, r, e] * s2
        return 0

    lax.fori_loop(0, C // 8, first_half, 0)

    gp_parts = jnp.concatenate(parts2(gp_ref[...]), axis=0)
    back = dot(oh_ref[SL:EXT, :], gp_parts, NT)
    bsend[...] = back[:, 0:C] + back[:, C:2 * C]
    returns = [copy(bsend.at[faces[f]], brecv.at[faces[f]], 10 + f, (xm, xp, ym, yp)[f]) for f in range(4)]
    for item in returns:
        item.start()
    for lt in range(3):
        i = pl.ds(lt * 128, 128)
        for pair in range(2):
            edges = [pl.ds((2 * pair + kk) * SL + lt * 128, 128) for kk in range(2)]

            def step(cb, carry, i=i, edges=edges):
                r = pl.ds(pl.multiple_of(cb * 8, 8), 8)
                carry = list(carry)
                g0 = gb_ref[r, i]
                g = [acc1_ref[m, r, i] * (g0 + g0) for m in range(8)]
                for kk, e in enumerate(edges):
                    p = p_ref[r, e]
                    slope = rp_ref[0, r, e] * g0 + rp_ref[1, r, e] * s_ref[0, r, e] + rp_ref[2, r, e] * s_ref[1, r, e]
                    t1, t2 = r_ref[1, r, e] * p, r_ref[2, r, e] * p
                    at = kk * 9
                    for m in range(8):
                        carry[at + m] = carry[at + m] + g[m] * (t1 if m < 3 else t2)
                    carry[at + 8] = carry[at + 8] + p * slope
                return tuple(carry)

            done = lax.fori_loop(0, C // 8, step, tuple(jnp.zeros((8, 128), F32) for _ in range(18)))
            for kk, e in enumerate(edges):
                for m in range(9):
                    gy_ref[m, :, e] = done[kk * 9 + m]

    stay = dot(oh_ref[0:SL, :], gp_parts, NT)
    g_p = stay[:, 0:C] + stay[:, C:2 * C]
    pl.semaphore_wait(know, 2)
    for item in shares:
        item.wait()
    mine = z * 2 + core
    column[mine] = jnp.sum(plane[...], axis=0)
    shares = [copy(column.at[mine], column.at[mine], 33 + n, there) for n, there in enumerate(column_partners)]
    for item in shares:
        item.start()
    for item in returns:
        item.wait()
    came = dot(soh_ref[...], jnp.concatenate(parts2(brecv[...]), axis=1))
    g_p = g_p + (came[:, 0:C] + came[:, C:2 * C])
    g_h1 = weight_dot(up1_n, g_p, NT) + (read_col[0] + read_col[1])
    g_b = weight_dot(mix_n[0], slope0 * g_h1)

    for m in range(9):
        g = acc0_ref[m - 1] * (g_b + g_b) if m else g_b
        v_ref[m] = weight_dot(low_n[DEGREE[m]], g)
    for lt in range(3):
        i = pl.ds(lt * 128, 128)
        for k in range(NE):
            e = pl.ds(k * SL + lt * 128, 128)
            y = [y_ref[m, :, e] for m in range(8)]
            sums = [gy_ref[m, :, e] for m in range(8)]
            slope = None
            for q in range(5):
                b = bs_ref[q, :, e]
                mixed = v_ref[0, q * 8:(q + 1) * 8, i]
                for m in range(8):
                    v = v_ref[m + 1, q * 8:(q + 1) * 8, i]
                    sums[m] = sums[m] + b * v
                    mixed = mixed + y[m] * v
                slope = b * mixed if slope is None else slope + b * mixed
            for m in range(8):
                gy_ref[m, :, e] = sums[m]
            gy_ref[8, :, e] = gy_ref[8, :, e] - gamma_col[0] * slope

    def summed(m):
        return jnp.sum(gy_ref[m], axis=0, keepdims=True)

    g1, g2, g3, g4, g5, g6, g7, g8 = [summed(m) for m in range(8)]
    g_sq = summed(8)
    rx, ry, rz, sq = [tail_ref[d][0:1, :] for d in range(4)]
    inv = lax.rsqrt(1.0 + sq)
    ux, uy, uz = rx * inv, ry * inv, rz * inv
    gux = R3 * g1 + R15 * (uy * g4 + uz * g7 + ux * g8) - R5 * (ux * g6)
    guy = R3 * g2 + R15 * (ux * g4 + uz * g5 - uy * g8) - R5 * (uy * g6)
    guz = R3 * g3 + R15 * (uy * g5 + ux * g7) + (2.0 * R5) * (uz * g6)
    twice = 2.0 * g_sq - (gux * rx + guy * ry + guz * rz) * (inv * inv * inv)
    g_edge = [gux * inv + twice * rx, guy * inv + twice * ry, guz * inv + twice * rz]
    row8 = lax.broadcasted_iota(jnp.int32, (8, E), 0)
    edge8 = jnp.where(row8 == 0, g_edge[0], jnp.where(row8 == 1, g_edge[1], jnp.where(row8 == 2, g_edge[2], 0.0)))
    edge24 = stack3(edge8)
    away = fold3(dot(edge24, oh_ref[SL:EXT, :], NT))
    fsend[0] = away[:, 0:128]
    fsend[1] = away[:, 128:256]
    lasts = [copy(fsend.at[f // 2], frecv.at[f], 14 + f, (xm, xp, ym, yp)[f]) for f in range(4)]
    for item in lasts:
        item.start()
    own = fold3(dot(edge24, oh_ref[0:SL, :], NT))
    for k in range(NE):
        own = own - edge8[:, k * SL:(k + 1) * SL]
    for item in lasts:
        item.wait()
    back8 = jnp.concatenate([jnp.where(low, frecv[0], frecv[1]), jnp.where(low, frecv[2], frecv[3])], axis=1)
    own = own + fold3(dot(stack3(back8), soh_ref[...], NT))
    force_out[...] = -own[0:3, :]
    for item in shares:
        item.wait()
    both = jnp.sum(column[...], axis=0)
    total = jnp.sum(jnp.where(low1, both, 0.0), axis=1, keepdims=True)
    number = jnp.sum(jnp.where(low1, 0.0, both), axis=1, keepdims=True)
    energy_out[0] = jnp.sum(total / number)


def shards(old_pos, old_species, block_dest, block_count, send_list, neighbours, embed, atom_ref,
           w_up, gammas, w_rad, w_mix, readout):
    vmem = pl.BlockSpec(memory_space=pltpu.VMEM)
    smem = pl.BlockSpec(memory_space=pltpu.SMEM)
    forces, energy = pl.pallas_call(
        body,
        name="potential",
        out_shape=(jax.ShapeDtypeStruct((3, SL), F32), jax.ShapeDtypeStruct((1,), F32)),
        in_specs=[pl.BlockSpec(memory_space=pltpu.HBM)] * 13,
        out_specs=(vmem, smem),
        scratch_shapes=[
            pltpu.VMEM((3, 2 * BLK), F32),
            pltpu.VMEM((2 * BLK,), jnp.int32),
            pltpu.SMEM((1, 2), jnp.int32),
            pltpu.SMEM((2,), jnp.int32),
            pltpu.VMEM((4, GH), jnp.int32),
            pltpu.VMEM((NE, SL), jnp.int32),
            pltpu.VMEM((5, C), F32),
            pltpu.SMEM((5,), F32),
            pltpu.VMEM((2, C, C), F32),
            pltpu.SMEM((2, 8), F32),
            pltpu.VMEM((2, 8, 3 * C), F32),
            pltpu.VMEM((2, C, C), F32),
            pltpu.VMEM((2, C), F32),
            pltpu.VMEM((8, 2 * BLK), F32),
            pltpu.VMEM((2, 8, BLK), F32),
            pltpu.VMEM((2, 8, BLK), F32),
            pltpu.VMEM((8, SL), F32),
            pltpu.VMEM((4, 8, E), F32),
            pltpu.VMEM((2, 8, 128), F32),
            pltpu.VMEM((4, 8, 128), F32),
            pltpu.VMEM((8, C), F32),
            pltpu.VMEM((EXT, E), BF16),
            pltpu.VMEM((SL, NG), BF16),
            pltpu.VMEM((8, 8, E), F32),
            pltpu.VMEM((5, 8, E), F32),
            pltpu.VMEM((40, 9 * SL), F32),
            pltpu.VMEM((3, C, E), F32),
            pltpu.VMEM((3, C, E), F32),
            pltpu.VMEM((C, E), F32),
            pltpu.VMEM((C, E), F32),
            pltpu.VMEM((8, C, SL), F32),
            pltpu.VMEM((8, C, SL), F32),
            pltpu.VMEM((C, SL), F32),
            pltpu.VMEM((C, SL), F32),
            pltpu.VMEM((9, 40, SL), F32),
            pltpu.VMEM((2, C, E), F32),
            pltpu.VMEM((NG, C), F32),
            pltpu.VMEM((NG, C), F32),
            pltpu.VMEM((NG, C), F32),
            pltpu.VMEM((NG, C), F32),
            pltpu.VMEM((2, 8, 128), F32),
            pltpu.VMEM((4, 8, 128), F32),
            pltpu.VMEM((9, 8, E), F32),
            pltpu.VMEM((16, 1, 128), F32),
            pltpu.VMEM((32, 1, 128), F32),
            pltpu.SemaphoreType.DMA((13,)),
            pltpu.SemaphoreType.REGULAR,
            pltpu.SemaphoreType.DMA((64,)),
            pltpu.SemaphoreType.DMA((64,)),
        ],
        compiler_params=pltpu.CompilerParams(collective_id=0, has_side_effects=True, vmem_limit_bytes=40 * 1024 * 1024),
    )(*[pltpu.with_memory_space_constraint(x, pltpu.HBM) for x in (
        old_pos, old_species, block_dest.T, block_count, send_list, neighbours, embed, atom_ref,
        w_up, gammas, w_rad, w_mix, readout)])
    return forces, energy.reshape(())


def solution(mesh):
    both = ("gx", "yz")
    return jax.shard_map(
        shards,
        mesh=mesh,
        in_specs=(
            P(None, both), P(both), P(both, None), P(both), P(both, None), P(None, both),
            P(), P(), P(), P(), P(), P(), P(),
        ),
        out_specs=(P(None, both), P()),
        check_vma=False,
    )
```

```python
import math

import jax
import jax.numpy as jnp
from jax import lax
from jax.experimental import pallas as pl
from jax.experimental.pallas import tpu as pltpu
from jax.sharding import PartitionSpec as P

MESH = pl.DeviceIdType.MESH
F32 = jnp.float32
BF16 = jnp.bfloat16

R3 = math.sqrt(3.0)
R15 = math.sqrt(15.0)
R5 = math.sqrt(5.0)
DEGREE = (0, 1, 1, 1, 2, 2, 2, 2, 2)

C = 128
NE = 4
BLK = 128
SL = 384
GH = 64
NG = 4 * GH
EXT = SL + NG
E = NE * SL
NN = (((1,), (0,)), ((), ()))
NT = (((1,), (1,)), ((), ()))
TN = (((0,), (0,)), ((), ()))


def dot(a, b, dims=NN):
    return lax.dot_general(a, b, dims, preferred_element_type=F32)


def head(x):
    return x.astype(BF16).astype(F32)


def parts2(x):
    hi = x.astype(BF16)
    return hi, (x - hi.astype(F32)).astype(BF16)


def stack3(x):
    hi = head(x)
    mid = head(x - hi)
    return jnp.concatenate([hi, mid, x - hi - mid], axis=0).astype(BF16)


def fold3(x):
    return x[0:8] + x[8:16] + x[16:24]


def weight_lhs(w):
    hi = head(w)
    low = jnp.concatenate([w - hi, jnp.zeros_like(w)], axis=1)
    return jnp.concatenate([jnp.concatenate([hi, hi], axis=1), low], axis=0).astype(BF16)


def weight_dot(lhs, x, dims=NN):
    out = dot(lhs, jnp.concatenate(parts2(x), axis=0 if dims is NN else 1), dims)
    half = lhs.shape[0] // 2
    return out[0:half] + out[half:]


def body(
    pos_hbm, species_hbm, dest_hbm, count_hbm, list_hbm, near_hbm, embed_hbm, atom_hbm, up_hbm, gamma_hbm,
    rad_hbm, mix_hbm, read_hbm,
    force_out, energy_out,
    pos_in, species_in, dest_in, count_in, list_in, near_in, embed_in, atom_in, up_in, gamma_in,
    rad_in, mix_in, read_in,
    tile_ref, mig_send, mig_recv, a_ref, tail_ref, gsend, grecv, emb_ref,
    oh_ref, soh_ref, y_ref, bs_ref, z_ref, r_ref, rp_ref, p_ref, gp_ref, acc0_ref, acc1_ref, b_ref, gb_ref, v_ref, s_ref,
    psend, precv, bsend, brecv, fsend, frecv, gy_ref, plane, column, load_sem, know, send_sem, recv_sem,
):
    gx, yz = lax.axis_index("gx"), lax.axis_index("yz")
    n_gx, n_yz = lax.axis_size("gx"), lax.axis_size("yz")
    xp = (lax.rem(gx + 1, n_gx), yz)
    xm = (lax.rem(gx + n_gx - 1, n_gx), yz)
    yp = (gx, lax.rem(yz + 1, n_yz))
    ym = (gx, lax.rem(yz + n_yz - 1, n_yz))

    x_lo, z, core = yz // 32, lax.rem(yz // 2, 16), lax.rem(yz, 2)

    def along(dz, dc):
        return (gx, x_lo * 32 + lax.rem(z + dz + 16, 16) * 2 + lax.rem(core + dc, 2))

    plane_partners = [
        (lax.rem(gx + d, n_gx), lax.rem(x_lo + b, 2) * 32 + z * 2 + core)
        for d in (1, 7, 6, 2, 5, 3, 4, 0) for b in (1, 0) if d or b
    ]
    far_first = (8, 7, 9, 6, 10, 5, 11, 4, 12, 3, 13, 2, 14, 1, 15, 0)
    column_partners = [along(dz, dc) for dz in far_first for dc in range(2) if dz or dc]
    relays = [along(4, 0), along(-4, 0)]

    barrier = pltpu.get_barrier_semaphore()
    greeted = [yp, ym] + plane_partners
    greeted += [along(dz, dc) for dz in (0, 1, -1, 2, -2, 3, -3, 4, -4) for dc in range(2) if dz or dc]

    def greet(those):
        for there in those:
            pl.semaphore_signal(barrier, inc=1, device_id=there, device_id_type=MESH)

    greet(greeted[0:4])
    loads = {}
    for n, (src, dst) in enumerate((
        (pos_hbm, pos_in), (species_hbm, species_in), (dest_hbm, dest_in), (count_hbm, count_in),
        (list_hbm, list_in), (near_hbm, near_in), (embed_hbm, embed_in), (up_hbm, up_in),
        (rad_hbm, rad_in), (gamma_hbm, gamma_in), (mix_hbm, mix_in), (read_hbm, read_in), (atom_hbm, atom_in),
    )):
        loads[n] = pltpu.make_async_copy(src, dst, load_sem.at[n])
        loads[n].start()
    greet(greeted[4:])

    def copy(src, dst, number, there):
        return pltpu.make_async_remote_copy(
            src_ref=src, dst_ref=dst, send_sem=send_sem.at[number], recv_sem=recv_sem.at[number],
            device_id=there, device_id_type=MESH,
        )

    sub = lax.broadcasted_iota(jnp.int32, (8, 128), 0)
    lane = lax.broadcasted_iota(jnp.int32, (8, 128), 1)

    for n in range(4):
        loads[n].wait()
    for b in range(2):
        kinds = jnp.broadcast_to(species_in[b * BLK:(b + 1) * BLK].reshape(1, BLK), (8, BLK))
        here = (kinds == sub - 3) & (lane < count_in[b])
        tile_ref[:, b * BLK:(b + 1) * BLK] = jnp.where(here, 1.0, 0.0).astype(F32)
    tile_ref[0:3, :] = pos_in[...]
    first, second = tile_ref[:, 0:BLK], tile_ref[:, BLK:2 * BLK]

    def packed(d):
        return jnp.where(dest_in[0, 0] == d, first, jnp.where(dest_in[0, 1] == d, second, 0.0))

    mig_send[0] = packed(0)
    mig_send[1] = packed(2)
    a_ref[:, BLK:2 * BLK] = packed(1)
    pl.semaphore_wait(barrier, len(greeted))
    moves = [copy(mig_send.at[0], mig_recv.at[0], 0, ym), copy(mig_send.at[1], mig_recv.at[1], 1, yp)]
    for move in moves:
        move.start()
    for there in relays:
        pl.semaphore_signal(know, inc=1, device_id=there, device_id_type=MESH)

    loads[4].wait()
    for pair in range(2):
        row = jnp.concatenate([list_in[2 * pair:2 * pair + 1, :], list_in[2 * pair + 1:2 * pair + 2, :]], axis=1)
        at = lax.broadcasted_iota(jnp.int32, (SL, 128), 0)
        soh_ref[:, pair * 128:(pair + 1) * 128] = jnp.where(at == row, 1.0, 0.0).astype(BF16)
    loads[5].wait()
    for k in range(NE):
        row = near_in[k:k + 1, :]

        def fill(block, _, row=row, k=k):
            base = pl.multiple_of(block * 128, 128)
            at = lax.broadcasted_iota(jnp.int32, (128, SL), 0) + base
            oh_ref[pl.ds(base, 128), k * SL:(k + 1) * SL] = jnp.where(at == row, 1.0, 0.0).astype(BF16)
            return 0

        lax.fori_loop(0, EXT // 128, fill, 0)

    for move in moves:
        move.wait()
    a_ref[:, 0:BLK] = mig_recv[0]
    a_ref[:, 2 * BLK:3 * BLK] = mig_recv[1]

    atoms = a_ref[...]
    atoms24 = stack3(atoms)
    picked = fold3(dot(atoms24, soh_ref[...]))
    gsend[0] = picked[:, 0:128]
    gsend[1] = picked[:, 128:256]
    ghosts = [copy(gsend.at[f // 2], grecv.at[f], 2 + f, (xp, xm, yp, ym)[f]) for f in range(4)]
    for ghost in ghosts:
        ghost.start()

    for n in range(6, 13):
        loads[n].wait()
    row_of = lax.broadcasted_iota(jnp.int32, (8, SL), 0)
    marks = jnp.where(row_of >= 3, atoms, 0.0)
    live = jnp.sum(marks, axis=0, keepdims=True)
    marks24 = jnp.concatenate([marks, marks, marks], axis=0).astype(BF16)
    near_local = fold3(dot(atoms24, oh_ref[0:SL, :]))

    emb_ref[...] = jnp.zeros((8, C), F32)
    emb_ref[3:8, :] = embed_in[...]
    h0 = dot(stack3(emb_ref[...]), marks24, TN)
    table = weight_dot(weight_lhs(emb_ref[...]), up_in[0])
    mix_t = [weight_lhs(mix_in[t].T) for t in range(2)]
    mix_n = [weight_lhs(mix_in[t]) for t in range(2)]
    up1_t = weight_lhs(up_in[1].T)
    up1_n = weight_lhs(up_in[1])
    reads = jnp.concatenate([read_in[...], jnp.zeros((6, C), F32)], axis=0).T
    read_col = [jnp.broadcast_to(reads[:, t:t + 1], (C, SL)) for t in range(2)]

    low_n, low_t = [], []
    for l in range(3):
        part = rad_in[0, :, l * C:(l + 1) * C]
        rows = jnp.concatenate([part * table[3 + q:4 + q, :] for q in range(5)], axis=0)
        hi = head(rows)
        low_n.append(weight_lhs(rows))
        low_t.append(jnp.concatenate([hi, hi, rows - hi, jnp.zeros((8, C), F32)], axis=0).T.astype(BF16))
    hi = head(rad_in[1])
    rad24 = jnp.concatenate([hi, hi, rad_in[1] - hi], axis=0).astype(BF16)

    def upright(values):
        out = jnp.zeros((8, 128), F32)
        for q in range(len(values)):
            if values[q] is not None:
                out = jnp.where(sub == q, values[q], out)
        return out

    gamma_col = [upright([gamma_in[t, q] for q in range(8)]) for t in range(2)]
    atom_col = upright([None, None, None] + [atom_in[q] for q in range(5)])

    for ghost in ghosts:
        ghost.wait()
    low = lane < GH
    ghost8 = jnp.concatenate([jnp.where(low, grecv[0], grecv[1]), jnp.where(low, grecv[2], grecv[3])], axis=1)
    near = near_local + fold3(dot(stack3(ghost8), oh_ref[SL:EXT, :]))

    def spread(rows, d):
        return jnp.broadcast_to(rows[d:d + 1, :], (8, rows.shape[1]))

    def offsets():
        out = []
        for d in range(3):
            there = spread(atoms, d)
            out.append(spread(near, d) - jnp.concatenate([there] * NE, axis=1))
        return out

    rx, ry, rz = offsets()
    sq = rx * rx + ry * ry + rz * rz
    inv = lax.rsqrt(1.0 + sq)
    ux, uy, uz = rx * inv, ry * inv, rz * inv
    y_ref[0] = R3 * ux
    y_ref[1] = R3 * uy
    y_ref[2] = R3 * uz
    y_ref[3] = R15 * ux * uy
    y_ref[4] = R15 * uy * uz
    y_ref[5] = (0.5 * R5) * (2.0 * uz * uz - ux * ux - uy * uy)
    y_ref[6] = R15 * ux * uz
    y_ref[7] = (0.5 * R15) * (ux * ux - uy * uy)
    for d, value in enumerate((rx, ry, rz, sq)):
        tail_ref[d] = value

    def basis(t):
        cols = jnp.concatenate([gamma_col[t]] * (E // 128), axis=1)
        return cols, 0.25 * jnp.exp(-cols * tail_ref[3])

    basis0 = basis(0)[1]
    for q in range(5):
        bs_ref[q] = basis0 * spread(near, 3 + q)

    for q in range(5):
        for lt in range(3):
            acc = [None] * 9
            for k in range(NE):
                e = pl.ds(k * SL + lt * 128, 128)
                b = bs_ref[q, :, e]
                for m in range(9):
                    value = b * y_ref[m - 1, :, e] if m else b
                    acc[m] = value if acc[m] is None else acc[m] + value
            for m in range(9):
                z_ref[q * 8:(q + 1) * 8, m * SL + lt * 128:m * SL + (lt + 1) * 128] = acc[m]

    total = None
    for m in range(9):
        block = z_ref[:, m * SL:(m + 1) * SL]
        hi = head(block)
        rows = jnp.concatenate([hi, block - hi, hi, jnp.zeros((8, SL), F32)], axis=0).astype(BF16)
        value = dot(low_t[DEGREE[m]], rows)
        if m:
            acc0_ref[m - 1] = value
        total = value * value + total if m else value
    mixed0 = weight_dot(mix_t[0], total)
    gate0 = 1.0 / (1.0 + jnp.exp(-mixed0))
    h1 = live * (h0 + mixed0 * gate0)

    p1 = weight_dot(up1_t, h1)
    p1_parts = jnp.concatenate(parts2(p1), axis=0)
    sent = dot(p1_parts, soh_ref[...])
    psend[...] = (sent[0:C] + sent[C:2 * C]).T
    faces = [pl.ds(f * GH, GH) for f in range(4)]
    outs = [copy(psend.at[faces[f]], precv.at[faces[f]], 6 + f, (xp, xm, yp, ym)[f]) for f in range(4)]
    for out in outs:
        out.start()

    slope0 = live * (gate0 * (1.0 + mixed0 * (1.0 - gate0)))

    def radial(values, out_ref):
        hi = head(values)
        rows = jnp.concatenate([hi, values - hi, hi], axis=0).astype(BF16)
        for l in range(3):
            out_ref[l] = dot(rad24[:, l * C:(l + 1) * C], rows, TN)

    cols1, basis1 = basis(1)
    radial(basis1, r_ref)
    radial(-cols1 * basis1, rp_ref)
    local1 = dot(p1_parts, oh_ref[0:SL, :])
    p_ref[...] = local1[0:C] + local1[C:2 * C]

    for out in outs:
        out.wait()
    ghost1 = dot(jnp.concatenate(parts2(precv[...].T), axis=0), oh_ref[SL:EXT, :])
    p_ref[...] = p_ref[...] + (ghost1[0:C] + ghost1[C:2 * C])

    def forward(cb, _):
        r = pl.ds(pl.multiple_of(cb * 8, 8), 8)
        for lt in range(3):
            acc = [None] * 9
            for k in range(NE):
                e = pl.ds(k * SL + lt * 128, 128)
                p = p_ref[r, e]
                terms = [r_ref[l, r, e] * p for l in range(3)]
                for m in range(9):
                    value = terms[DEGREE[m]]
                    if m:
                        value = value * y_ref[m - 1, :, e]
                    acc[m] = value if acc[m] is None else acc[m] + value
            i = pl.ds(lt * 128, 128)
            total = acc[0]
            for m in range(1, 9):
                acc1_ref[m - 1, r, i] = acc[m]
                total = total + acc[m] * acc[m]
            b_ref[r, i] = total
        return 0

    lax.fori_loop(0, C // 8, forward, 0)
    mixed1 = weight_dot(mix_t[1], b_ref[...])
    gate1 = 1.0 / (1.0 + jnp.exp(-mixed1))
    h2 = live * (h1 + mixed1 * gate1)
    value = h1 * read_col[0] + h2 * read_col[1]
    rows = jnp.sum(value, axis=0, keepdims=True)
    cols3 = jnp.concatenate([atom_col] * 3, axis=1)
    rows = rows + jnp.sum(marks * cols3, axis=0, keepdims=True)
    row_e = rows[:, 0:128] + rows[:, 128:256] + rows[:, 256:384]
    row_n = live[:, 0:128] + live[:, 128:256] + live[:, 256:384]
    low1 = lax.broadcasted_iota(jnp.int32, (1, 128), 1) < 64
    row_e = row_e + pltpu.roll(row_e, 64, 1)
    row_n = row_n + pltpu.roll(row_n, 64, 1)
    mine = gx * 2 + x_lo
    plane[mine] = jnp.where(low1, row_e, row_n)
    shares = [copy(plane.at[mine], plane.at[mine], 18 + n, there) for n, there in enumerate(plane_partners)]
    for item in shares:
        item.start()

    slope1 = live * (gate1 * (1.0 + mixed1 * (1.0 - gate1)))
    gb_ref[...] = weight_dot(mix_n[1], slope1 * read_col[1])
    def first_half(cb, _):
        r = pl.ds(pl.multiple_of(cb * 8, 8), 8)
        for lt in range(3):
            i = pl.ds(lt * 128, 128)
            g0 = gb_ref[r, i]
            g = [g0] + [acc1_ref[m, r, i] * (g0 + g0) for m in range(8)]
            for k in range(NE):
                e = pl.ds(k * SL + lt * 128, 128)
                y = [y_ref[m, :, e] for m in range(8)]
                s1 = g[1] * y[0] + g[2] * y[1] + g[3] * y[2]
                s2 = g[4] * y[3] + g[5] * y[4] + g[6] * y[5] + g[7] * y[6] + g[8] * y[7]
                s_ref[0, r, e] = s1
                s_ref[1, r, e] = s2
                gp_ref[r, e] = r_ref[0, r, e] * g0 + r_ref[1, r, e] * s1 + r_ref[2, r, e] * s2
        return 0

    lax.fori_loop(0, C // 8, first_half, 0)

    gp_parts = jnp.concatenate(parts2(gp_ref[...]), axis=0)
    back = dot(oh_ref[SL:EXT, :], gp_parts, NT)
    bsend[...] = back[:, 0:C] + back[:, C:2 * C]
    returns = [copy(bsend.at[faces[f]], brecv.at[faces[f]], 10 + f, (xm, xp, ym, yp)[f]) for f in range(4)]
    for item in returns:
        item.start()
    for lt in range(3):
        i = pl.ds(lt * 128, 128)
        for pair in range(2):
            edges = [pl.ds((2 * pair + kk) * SL + lt * 128, 128) for kk in range(2)]

            def step(cb, carry, i=i, edges=edges):
                r = pl.ds(pl.multiple_of(cb * 8, 8), 8)
                carry = list(carry)
                g0 = gb_ref[r, i]
                g = [acc1_ref[m, r, i] * (g0 + g0) for m in range(8)]
                for kk, e in enumerate(edges):
                    p = p_ref[r, e]
                    slope = rp_ref[0, r, e] * g0 + rp_ref[1, r, e] * s_ref[0, r, e] + rp_ref[2, r, e] * s_ref[1, r, e]
                    t1, t2 = r_ref[1, r, e] * p, r_ref[2, r, e] * p
                    at = kk * 9
                    for m in range(8):
                        carry[at + m] = carry[at + m] + g[m] * (t1 if m < 3 else t2)
                    carry[at + 8] = carry[at + 8] + p * slope
                return tuple(carry)

            done = lax.fori_loop(0, C // 8, step, tuple(jnp.zeros((8, 128), F32) for _ in range(18)))
            for kk, e in enumerate(edges):
                for m in range(9):
                    gy_ref[m, :, e] = done[kk * 9 + m]

    stay = dot(oh_ref[0:SL, :], gp_parts, NT)
    g_p = stay[:, 0:C] + stay[:, C:2 * C]
    pl.semaphore_wait(know, 2)
    for item in shares:
        item.wait()
    mine = z * 2 + core
    column[mine] = jnp.sum(plane[...], axis=0)
    shares = [copy(column.at[mine], column.at[mine], 33 + n, there) for n, there in enumerate(column_partners)]
    for item in shares:
        item.start()
    for item in returns:
        item.wait()
    came = dot(soh_ref[...], jnp.concatenate(parts2(brecv[...]), axis=1))
    g_p = g_p + (came[:, 0:C] + came[:, C:2 * C])
    g_h1 = weight_dot(up1_n, g_p, NT) + (read_col[0] + read_col[1])
    g_b = weight_dot(mix_n[0], slope0 * g_h1)

    for m in range(9):
        g = acc0_ref[m - 1] * (g_b + g_b) if m else g_b
        v_ref[m] = weight_dot(low_n[DEGREE[m]], g)
    for lt in range(3):
        i = pl.ds(lt * 128, 128)
        for k in range(NE):
            e = pl.ds(k * SL + lt * 128, 128)
            y = [y_ref[m, :, e] for m in range(8)]
            sums = [gy_ref[m, :, e] for m in range(8)]
            slope = None
            for q in range(5):
                b = bs_ref[q, :, e]
                mixed = v_ref[0, q * 8:(q + 1) * 8, i]
                for m in range(8):
                    v = v_ref[m + 1, q * 8:(q + 1) * 8, i]
                    sums[m] = sums[m] + b * v
                    mixed = mixed + y[m] * v
                slope = b * mixed if slope is None else slope + b * mixed
            for m in range(8):
                gy_ref[m, :, e] = sums[m]
            gy_ref[8, :, e] = gy_ref[8, :, e] - gamma_col[0] * slope

    def summed(m):
        return jnp.sum(gy_ref[m], axis=0, keepdims=True)

    g1, g2, g3, g4, g5, g6, g7, g8 = [summed(m) for m in range(8)]
    g_sq = summed(8)
    rx, ry, rz, sq = [tail_ref[d][0:1, :] for d in range(4)]
    inv = lax.rsqrt(1.0 + sq)
    ux, uy, uz = rx * inv, ry * inv, rz * inv
    gux = R3 * g1 + R15 * (uy * g4 + uz * g7 + ux * g8) - R5 * (ux * g6)
    guy = R3 * g2 + R15 * (ux * g4 + uz * g5 - uy * g8) - R5 * (uy * g6)
    guz = R3 * g3 + R15 * (uy * g5 + ux * g7) + (2.0 * R5) * (uz * g6)
    twice = 2.0 * g_sq - (gux * rx + guy * ry + guz * rz) * (inv * inv * inv)
    g_edge = [gux * inv + twice * rx, guy * inv + twice * ry, guz * inv + twice * rz]
    row8 = lax.broadcasted_iota(jnp.int32, (8, E), 0)
    edge8 = jnp.where(row8 == 0, g_edge[0], jnp.where(row8 == 1, g_edge[1], jnp.where(row8 == 2, g_edge[2], 0.0)))
    edge24 = stack3(edge8)
    away = fold3(dot(edge24, oh_ref[SL:EXT, :], NT))
    fsend[0] = away[:, 0:128]
    fsend[1] = away[:, 128:256]
    lasts = [copy(fsend.at[f // 2], frecv.at[f], 14 + f, (xm, xp, ym, yp)[f]) for f in range(4)]
    for item in lasts:
        item.start()
    own = fold3(dot(edge24, oh_ref[0:SL, :], NT))
    for k in range(NE):
        own = own - edge8[:, k * SL:(k + 1) * SL]
    for item in lasts:
        item.wait()
    back8 = jnp.concatenate([jnp.where(low, frecv[0], frecv[1]), jnp.where(low, frecv[2], frecv[3])], axis=1)
    own = own + fold3(dot(stack3(back8), soh_ref[...], NT))
    force_out[...] = -own[0:3, :]
    for item in shares:
        item.wait()
    both = jnp.sum(column[...], axis=0)
    total = jnp.sum(jnp.where(low1, both, 0.0), axis=1, keepdims=True)
    number = jnp.sum(jnp.where(low1, 0.0, both), axis=1, keepdims=True)
    energy_out[...] = jnp.broadcast_to(total / number, (8, 128))


def shards(old_pos, old_species, block_dest, block_count, send_list, neighbours, embed, atom_ref,
           w_up, gammas, w_rad, w_mix, readout):
    vmem = pl.BlockSpec(memory_space=pltpu.VMEM)
    forces, energy = pl.pallas_call(
        body,
        name="potential",
        out_shape=(jax.ShapeDtypeStruct((3, SL), F32), jax.ShapeDtypeStruct((8, 128), F32)),
        in_specs=[pl.BlockSpec(memory_space=pltpu.HBM)] * 13,
        out_specs=(vmem, vmem),
        scratch_shapes=[
            pltpu.VMEM((3, 2 * BLK), F32),
            pltpu.VMEM((2 * BLK,), jnp.int32),
            pltpu.SMEM((1, 2), jnp.int32),
            pltpu.SMEM((2,), jnp.int32),
            pltpu.VMEM((4, GH), jnp.int32),
            pltpu.VMEM((NE, SL), jnp.int32),
            pltpu.VMEM((5, C), F32),
            pltpu.SMEM((5,), F32),
            pltpu.VMEM((2, C, C), F32),
            pltpu.SMEM((2, 8), F32),
            pltpu.VMEM((2, 8, 3 * C), F32),
            pltpu.VMEM((2, C, C), F32),
            pltpu.VMEM((2, C), F32),
            pltpu.VMEM((8, 2 * BLK), F32),
            pltpu.VMEM((2, 8, BLK), F32),
            pltpu.VMEM((2, 8, BLK), F32),
            pltpu.VMEM((8, SL), F32),
            pltpu.VMEM((4, 8, E), F32),
            pltpu.VMEM((2, 8, 128), F32),
            pltpu.VMEM((4, 8, 128), F32),
            pltpu.VMEM((8, C), F32),
            pltpu.VMEM((EXT, E), BF16),
            pltpu.VMEM((SL, NG), BF16),
            pltpu.VMEM((8, 8, E), F32),
            pltpu.VMEM((5, 8, E), F32),
            pltpu.VMEM((40, 9 * SL), F32),
            pltpu.VMEM((3, C, E), F32),
            pltpu.VMEM((3, C, E), F32),
            pltpu.VMEM((C, E), F32),
            pltpu.VMEM((C, E), F32),
            pltpu.VMEM((8, C, SL), F32),
            pltpu.VMEM((8, C, SL), F32),
            pltpu.VMEM((C, SL), F32),
            pltpu.VMEM((C, SL), F32),
            pltpu.VMEM((9, 40, SL), F32),
            pltpu.VMEM((2, C, E), F32),
            pltpu.VMEM((NG, C), F32),
            pltpu.VMEM((NG, C), F32),
            pltpu.VMEM((NG, C), F32),
            pltpu.VMEM((NG, C), F32),
            pltpu.VMEM((2, 8, 128), F32),
            pltpu.VMEM((4, 8, 128), F32),
            pltpu.VMEM((9, 8, E), F32),
            pltpu.VMEM((16, 1, 128), F32),
            pltpu.VMEM((32, 1, 128), F32),
            pltpu.SemaphoreType.DMA((13,)),
            pltpu.SemaphoreType.REGULAR,
            pltpu.SemaphoreType.DMA((64,)),
            pltpu.SemaphoreType.DMA((64,)),
        ],
        compiler_params=pltpu.CompilerParams(collective_id=0, has_side_effects=True, vmem_limit_bytes=40 * 1024 * 1024),
    )(*[pltpu.with_memory_space_constraint(x, pltpu.HBM) for x in (
        old_pos, old_species, block_dest.T, block_count, send_list, neighbours, embed, atom_ref,
        w_up, gammas, w_rad, w_mix, readout)])
    return forces, energy[0, 0]


def solution(mesh):
    both = ("gx", "yz")
    return jax.shard_map(
        shards,
        mesh=mesh,
        in_specs=(
            P(None, both), P(both), P(both, None), P(both), P(both, None), P(None, both),
            P(), P(), P(), P(), P(), P(), P(),
        ),
        out_specs=(P(None, both), P()),
        check_vma=False,
    )
```

```python
import math

import jax
import jax.numpy as jnp
from jax import lax
from jax.experimental import pallas as pl
from jax.experimental.pallas import tpu as pltpu
from jax.sharding import PartitionSpec as P

MESH = pl.DeviceIdType.MESH
F32 = jnp.float32
BF16 = jnp.bfloat16

R3 = math.sqrt(3.0)
R15 = math.sqrt(15.0)
R5 = math.sqrt(5.0)
DEGREE = (0, 1, 1, 1, 2, 2, 2, 2, 2)

C = 128
NE = 4
BLK = 128
SL = 384
GH = 64
NG = 4 * GH
EXT = SL + NG
E = NE * SL
NN = (((1,), (0,)), ((), ()))
NT = (((1,), (1,)), ((), ()))
TN = (((0,), (0,)), ((), ()))


def dot(a, b, dims=NN):
    return lax.dot_general(a, b, dims, preferred_element_type=F32)


def head(x):
    return x.astype(BF16).astype(F32)


def parts2(x):
    hi = x.astype(BF16)
    return hi, (x - hi.astype(F32)).astype(BF16)


def stack3(x):
    hi = head(x)
    mid = head(x - hi)
    return jnp.concatenate([hi, mid, x - hi - mid], axis=0).astype(BF16)


def fold3(x):
    return x[0:8] + x[8:16] + x[16:24]


def weight_lhs(w):
    hi = head(w)
    low = jnp.concatenate([w - hi, jnp.zeros_like(w)], axis=1)
    return jnp.concatenate([jnp.concatenate([hi, hi], axis=1), low], axis=0).astype(BF16)


def weight_dot(lhs, x, dims=NN):
    out = dot(lhs, jnp.concatenate(parts2(x), axis=0 if dims is NN else 1), dims)
    half = lhs.shape[0] // 2
    return out[0:half] + out[half:]


def body(
    pos_hbm, species_hbm, dest_hbm, count_hbm, list_hbm, near_hbm, embed_hbm, atom_hbm, up_hbm, gamma_hbm,
    rad_hbm, mix_hbm, read_hbm,
    force_out, energy_out,
    pos_in, species_in, dest_in, count_in, list_in, near_in, embed_in, atom_in, up_in, gamma_in,
    rad_in, mix_in, read_in,
    tile_ref, mig_send, mig_recv, a_ref, tail_ref, gsend, grecv, emb_ref,
    oh_ref, soh_ref, y_ref, bs_ref, z_ref, r_ref, rp_ref, p_ref, gp_ref, acc0_ref, acc1_ref, b_ref, gb_ref, v_ref, s_ref,
    psend, precv, bsend, brecv, fsend, frecv, gy_ref, plane, column, load_sem, know, send_sem, recv_sem,
):
    gx, yz = lax.axis_index("gx"), lax.axis_index("yz")
    n_gx, n_yz = lax.axis_size("gx"), lax.axis_size("yz")
    xp = (lax.rem(gx + 1, n_gx), yz)
    xm = (lax.rem(gx + n_gx - 1, n_gx), yz)
    yp = (gx, lax.rem(yz + 1, n_yz))
    ym = (gx, lax.rem(yz + n_yz - 1, n_yz))

    x_lo, z, core = yz // 32, lax.rem(yz // 2, 16), lax.rem(yz, 2)

    def along(dz, dc):
        return (gx, x_lo * 32 + lax.rem(z + dz + 16, 16) * 2 + lax.rem(core + dc, 2))

    plane_partners = [
        (lax.rem(gx + d, n_gx), lax.rem(x_lo + b, 2) * 32 + z * 2 + core)
        for d in (1, 7, 6, 2, 5, 3, 4, 0) for b in (1, 0) if d or b
    ]
    far_first = (8, 7, 9, 6, 10, 5, 11, 4, 12, 3, 13, 2, 14, 1, 15, 0)
    column_partners = [along(dz, dc) for dz in far_first for dc in range(2) if dz or dc]
    relays = [along(4, 0), along(-4, 0)]

    barrier = pltpu.get_barrier_semaphore()
    greeted = [yp, ym] + plane_partners
    greeted += [along(dz, dc) for dz in (0, 1, -1, 2, -2, 3, -3, 4, -4) for dc in range(2) if dz or dc]

    def greet(those):
        for there in those:
            pl.semaphore_signal(barrier, inc=1, device_id=there, device_id_type=MESH)

    greet(greeted[0:4])
    loads = {}
    for n, (src, dst) in enumerate((
        (pos_hbm, pos_in), (species_hbm, species_in), (dest_hbm, dest_in), (count_hbm, count_in),
        (list_hbm, list_in), (near_hbm, near_in), (embed_hbm, embed_in), (up_hbm, up_in),
        (rad_hbm, rad_in), (gamma_hbm, gamma_in), (mix_hbm, mix_in), (read_hbm, read_in), (atom_hbm, atom_in),
    )):
        loads[n] = pltpu.make_async_copy(src, dst, load_sem.at[n])
        loads[n].start()
    greet(greeted[4:])

    def copy(src, dst, number, there):
        return pltpu.make_async_remote_copy(
            src_ref=src, dst_ref=dst, send_sem=send_sem.at[number], recv_sem=recv_sem.at[number],
            device_id=there, device_id_type=MESH,
        )

    sub = lax.broadcasted_iota(jnp.int32, (8, 128), 0)
    lane = lax.broadcasted_iota(jnp.int32, (8, 128), 1)

    for n in range(4):
        loads[n].wait()
    for b in range(2):
        kinds = jnp.broadcast_to(species_in[b * BLK:(b + 1) * BLK].reshape(1, BLK), (8, BLK))
        here = (kinds == sub - 3) & (lane < count_in[b])
        tile_ref[:, b * BLK:(b + 1) * BLK] = jnp.where(here, 1.0, 0.0).astype(F32)
    tile_ref[0:3, :] = pos_in[...]
    first, second = tile_ref[:, 0:BLK], tile_ref[:, BLK:2 * BLK]

    def packed(d):
        return jnp.where(dest_in[0, 0] == d, first, jnp.where(dest_in[0, 1] == d, second, 0.0))

    mig_send[0] = packed(0)
    mig_send[1] = packed(2)
    a_ref[:, BLK:2 * BLK] = packed(1)
    pl.semaphore_wait(barrier, len(greeted))
    moves = [copy(mig_send.at[0], mig_recv.at[0], 0, ym), copy(mig_send.at[1], mig_recv.at[1], 1, yp)]
    for move in moves:
        move.start()
    for there in relays:
        pl.semaphore_signal(know, inc=1, device_id=there, device_id_type=MESH)

    loads[4].wait()
    for pair in range(2):
        row = jnp.concatenate([list_in[2 * pair:2 * pair + 1, :], list_in[2 * pair + 1:2 * pair + 2, :]], axis=1)
        at = lax.broadcasted_iota(jnp.int32, (SL, 128), 0)
        soh_ref[:, pair * 128:(pair + 1) * 128] = jnp.where(at == row, 1.0, 0.0).astype(BF16)
    loads[5].wait()
    for k in range(NE):
        row = near_in[k:k + 1, :]

        def fill(block, _, row=row, k=k):
            base = pl.multiple_of(block * 128, 128)
            at = lax.broadcasted_iota(jnp.int32, (128, SL), 0) + base
            oh_ref[pl.ds(base, 128), k * SL:(k + 1) * SL] = jnp.where(at == row, 1.0, 0.0).astype(BF16)
            return 0

        lax.fori_loop(0, EXT // 128, fill, 0)

    for move in moves:
        move.wait()
    a_ref[:, 0:BLK] = mig_recv[0]
    a_ref[:, 2 * BLK:3 * BLK] = mig_recv[1]

    atoms = a_ref[...]
    atoms24 = stack3(atoms)
    picked = fold3(dot(atoms24, soh_ref[...]))
    gsend[0] = picked[:, 0:128]
    gsend[1] = picked[:, 128:256]
    ghosts = [copy(gsend.at[f // 2], grecv.at[f], 2 + f, (xp, xm, yp, ym)[f]) for f in range(4)]
    for ghost in ghosts:
        ghost.start()

    for n in range(6, 13):
        loads[n].wait()
    row_of = lax.broadcasted_iota(jnp.int32, (8, SL), 0)
    marks = jnp.where(row_of >= 3, atoms, 0.0)
    live = jnp.sum(marks, axis=0, keepdims=True)
    marks24 = jnp.concatenate([marks, marks, marks], axis=0).astype(BF16)
    near_local = fold3(dot(atoms24, oh_ref[0:SL, :]))

    emb_ref[...] = jnp.zeros((8, C), F32)
    emb_ref[3:8, :] = embed_in[...]
    h0 = dot(stack3(emb_ref[...]), marks24, TN)
    table = weight_dot(weight_lhs(emb_ref[...]), up_in[0])
    mix_t = [weight_lhs(mix_in[t].T) for t in range(2)]
    mix_n = [weight_lhs(mix_in[t]) for t in range(2)]
    up1_t = weight_lhs(up_in[1].T)
    up1_n = weight_lhs(up_in[1])
    reads = jnp.concatenate([read_in[...], jnp.zeros((6, C), F32)], axis=0).T
    read_col = [jnp.broadcast_to(reads[:, t:t + 1], (C, SL)) for t in range(2)]

    low_n, low_t = [], []
    for l in range(3):
        part = rad_in[0, :, l * C:(l + 1) * C]
        rows = jnp.concatenate([part * table[3 + q:4 + q, :] for q in range(5)], axis=0)
        hi = head(rows)
        low_n.append(weight_lhs(rows))
        low_t.append(jnp.concatenate([hi, hi, rows - hi, jnp.zeros((8, C), F32)], axis=0).T.astype(BF16))
    hi = head(rad_in[1])
    rad24 = jnp.concatenate([hi, hi, rad_in[1] - hi], axis=0).astype(BF16)

    def upright(values):
        out = jnp.zeros((8, 128), F32)
        for q in range(len(values)):
            if values[q] is not None:
                out = jnp.where(sub == q, values[q], out)
        return out

    gamma_col = [upright([gamma_in[t, q] for q in range(8)]) for t in range(2)]
    atom_col = upright([None, None, None] + [atom_in[q] for q in range(5)])

    for ghost in ghosts:
        ghost.wait()
    low = lane < GH
    ghost8 = jnp.concatenate([jnp.where(low, grecv[0], grecv[1]), jnp.where(low, grecv[2], grecv[3])], axis=1)
    near = near_local + fold3(dot(stack3(ghost8), oh_ref[SL:EXT, :]))

    def spread(rows, d):
        return jnp.broadcast_to(rows[d:d + 1, :], (8, rows.shape[1]))

    def offsets():
        out = []
        for d in range(3):
            there = spread(atoms, d)
            out.append(spread(near, d) - jnp.concatenate([there] * NE, axis=1))
        return out

    rx, ry, rz = offsets()
    sq = rx * rx + ry * ry + rz * rz
    inv = lax.rsqrt(1.0 + sq)
    ux, uy, uz = rx * inv, ry * inv, rz * inv
    y_ref[0] = R3 * ux
    y_ref[1] = R3 * uy
    y_ref[2] = R3 * uz
    y_ref[3] = R15 * ux * uy
    y_ref[4] = R15 * uy * uz
    y_ref[5] = (0.5 * R5) * (2.0 * uz * uz - ux * ux - uy * uy)
    y_ref[6] = R15 * ux * uz
    y_ref[7] = (0.5 * R15) * (ux * ux - uy * uy)
    for d, value in enumerate((rx, ry, rz, sq)):
        tail_ref[d] = value

    def basis(t):
        cols = jnp.concatenate([gamma_col[t]] * (E // 128), axis=1)
        return cols, 0.25 * jnp.exp(-cols * tail_ref[3])

    basis0 = basis(0)[1]
    for q in range(5):
        bs_ref[q] = basis0 * spread(near, 3 + q)

    for q in range(5):
        for lt in range(3):
            acc = [None] * 9
            for k in range(NE):
                e = pl.ds(k * SL + lt * 128, 128)
                b = bs_ref[q, :, e]
                for m in range(9):
                    value = b * y_ref[m - 1, :, e] if m else b
                    acc[m] = value if acc[m] is None else acc[m] + value
            for m in range(9):
                z_ref[q * 8:(q + 1) * 8, m * SL + lt * 128:m * SL + (lt + 1) * 128] = acc[m]

    total = None
    for m in range(9):
        block = z_ref[:, m * SL:(m + 1) * SL]
        hi = head(block)
        rows = jnp.concatenate([hi, block - hi, hi, jnp.zeros((8, SL), F32)], axis=0).astype(BF16)
        value = dot(low_t[DEGREE[m]], rows)
        if m:
            acc0_ref[m - 1] = value
        total = value * value + total if m else value
    mixed0 = weight_dot(mix_t[0], total)
    gate0 = 1.0 / (1.0 + jnp.exp(-mixed0))
    h1 = live * (h0 + mixed0 * gate0)

    p1 = weight_dot(up1_t, h1)
    p1_parts = jnp.concatenate(parts2(p1), axis=0)
    sent = dot(p1_parts, soh_ref[...])
    psend[...] = (sent[0:C] + sent[C:2 * C]).T
    faces = [pl.ds(f * GH, GH) for f in range(4)]
    outs = [copy(psend.at[faces[f]], precv.at[faces[f]], 6 + f, (xp, xm, yp, ym)[f]) for f in range(4)]
    for out in outs:
        out.start()

    slope0 = live * (gate0 * (1.0 + mixed0 * (1.0 - gate0)))

    def radial(values, out_ref):
        hi = head(values)
        rows = jnp.concatenate([hi, values - hi, hi], axis=0).astype(BF16)
        for l in range(3):
            out_ref[l] = dot(rad24[:, l * C:(l + 1) * C], rows, TN)

    cols1, basis1 = basis(1)
    radial(basis1, r_ref)
    radial(-cols1 * basis1, rp_ref)
    local1 = dot(p1_parts, oh_ref[0:SL, :])
    p_ref[...] = local1[0:C] + local1[C:2 * C]

    for out in outs:
        out.wait()
    ghost1 = dot(jnp.concatenate(parts2(precv[...].T), axis=0), oh_ref[SL:EXT, :])
    p_ref[...] = p_ref[...] + (ghost1[0:C] + ghost1[C:2 * C])

    def forward(cb, _):
        r = pl.ds(pl.multiple_of(cb * 8, 8), 8)
        for lt in range(3):
            acc = [None] * 9
            for k in range(NE):
                e = pl.ds(k * SL + lt * 128, 128)
                p = p_ref[r, e]
                terms = [r_ref[l, r, e] * p for l in range(3)]
                for m in range(9):
                    value = terms[DEGREE[m]]
                    if m:
                        value = value * y_ref[m - 1, :, e]
                    acc[m] = value if acc[m] is None else acc[m] + value
            i = pl.ds(lt * 128, 128)
            total = acc[0]
            for m in range(1, 9):
                acc1_ref[m - 1, r, i] = acc[m]
                total = total + acc[m] * acc[m]
            b_ref[r, i] = total
        return 0

    lax.fori_loop(0, C // 8, forward, 0)
    mixed1 = weight_dot(mix_t[1], b_ref[...])
    gate1 = 1.0 / (1.0 + jnp.exp(-mixed1))
    h2 = live * (h1 + mixed1 * gate1)
    value = h1 * read_col[0] + h2 * read_col[1]
    rows = jnp.sum(value, axis=0, keepdims=True)
    cols3 = jnp.concatenate([atom_col] * 3, axis=1)
    rows = rows + jnp.sum(marks * cols3, axis=0, keepdims=True)
    row_e = rows[:, 0:128] + rows[:, 128:256] + rows[:, 256:384]
    row_n = live[:, 0:128] + live[:, 128:256] + live[:, 256:384]
    low1 = lax.broadcasted_iota(jnp.int32, (1, 128), 1) < 64
    row_e = row_e + pltpu.roll(row_e, 64, 1)
    row_n = row_n + pltpu.roll(row_n, 64, 1)
    mine = gx * 2 + x_lo
    plane[mine] = jnp.where(low1, row_e, row_n)
    shares = [copy(plane.at[mine], plane.at[mine], 18 + n, there) for n, there in enumerate(plane_partners)]
    for item in shares:
        item.start()

    slope1 = live * (gate1 * (1.0 + mixed1 * (1.0 - gate1)))
    gb_ref[...] = weight_dot(mix_n[1], slope1 * read_col[1])
    def first_half(cb, _):
        r = pl.ds(pl.multiple_of(cb * 8, 8), 8)
        for lt in range(3):
            i = pl.ds(lt * 128, 128)
            g0 = gb_ref[r, i]
            g = [g0] + [acc1_ref[m, r, i] * (g0 + g0) for m in range(8)]
            for k in range(NE):
                e = pl.ds(k * SL + lt * 128, 128)
                y = [y_ref[m, :, e] for m in range(8)]
                s1 = g[1] * y[0] + g[2] * y[1] + g[3] * y[2]
                s2 = g[4] * y[3] + g[5] * y[4] + g[6] * y[5] + g[7] * y[6] + g[8] * y[7]
                s_ref[0, r, e] = s1
                s_ref[1, r, e] = s2
                gp_ref[r, e] = r_ref[0, r, e] * g0 + r_ref[1, r, e] * s1 + r_ref[2, r, e] * s2
        return 0

    lax.fori_loop(0, C // 8, first_half, 0)

    gp_parts = jnp.concatenate(parts2(gp_ref[...]), axis=0)
    back = dot(oh_ref[SL:EXT, :], gp_parts, NT)
    bsend[...] = back[:, 0:C] + back[:, C:2 * C]
    returns = [copy(bsend.at[faces[f]], brecv.at[faces[f]], 10 + f, (xm, xp, ym, yp)[f]) for f in range(4)]
    for item in returns:
        item.start()
    for lt in range(3):
        i = pl.ds(lt * 128, 128)
        for pair in range(2):
            edges = [pl.ds((2 * pair + kk) * SL + lt * 128, 128) for kk in range(2)]

            def step(cb, carry, i=i, edges=edges):
                r = pl.ds(pl.multiple_of(cb * 8, 8), 8)
                carry = list(carry)
                g0 = gb_ref[r, i]
                g = [acc1_ref[m, r, i] * (g0 + g0) for m in range(8)]
                for kk, e in enumerate(edges):
                    p = p_ref[r, e]
                    slope = rp_ref[0, r, e] * g0 + rp_ref[1, r, e] * s_ref[0, r, e] + rp_ref[2, r, e] * s_ref[1, r, e]
                    t1, t2 = r_ref[1, r, e] * p, r_ref[2, r, e] * p
                    at = kk * 9
                    for m in range(8):
                        carry[at + m] = carry[at + m] + g[m] * (t1 if m < 3 else t2)
                    carry[at + 8] = carry[at + 8] + p * slope
                return tuple(carry)

            done = lax.fori_loop(0, C // 8, step, tuple(jnp.zeros((8, 128), F32) for _ in range(18)))
            for kk, e in enumerate(edges):
                for m in range(9):
                    gy_ref[m, :, e] = done[kk * 9 + m]

    stay = dot(oh_ref[0:SL, :], gp_parts, NT)
    g_p = stay[:, 0:C] + stay[:, C:2 * C]
    pl.semaphore_wait(know, 2)
    for item in shares:
        item.wait()
    mine = z * 2 + core
    column[mine] = jnp.sum(plane[...], axis=0)
    shares = [copy(column.at[mine], column.at[mine], 33 + n, there) for n, there in enumerate(column_partners)]
    for item in shares:
        item.start()
    for item in returns:
        item.wait()
    came = dot(soh_ref[...], jnp.concatenate(parts2(brecv[...]), axis=1))
    g_p = g_p + (came[:, 0:C] + came[:, C:2 * C])
    g_h1 = weight_dot(up1_n, g_p, NT) + (read_col[0] + read_col[1])
    g_b = weight_dot(mix_n[0], slope0 * g_h1)

    for m in range(9):
        g = acc0_ref[m - 1] * (g_b + g_b) if m else g_b
        v_ref[m] = weight_dot(low_n[DEGREE[m]], g)
    for lt in range(3):
        i = pl.ds(lt * 128, 128)
        for k in range(NE):
            e = pl.ds(k * SL + lt * 128, 128)
            y = [y_ref[m, :, e] for m in range(8)]
            sums = [gy_ref[m, :, e] for m in range(8)]
            slope = None
            for q in range(5):
                b = bs_ref[q, :, e]
                mixed = v_ref[0, q * 8:(q + 1) * 8, i]
                for m in range(8):
                    v = v_ref[m + 1, q * 8:(q + 1) * 8, i]
                    sums[m] = sums[m] + b * v
                    mixed = mixed + y[m] * v
                slope = b * mixed if slope is None else slope + b * mixed
            for m in range(8):
                gy_ref[m, :, e] = sums[m]
            gy_ref[8, :, e] = gy_ref[8, :, e] - gamma_col[0] * slope

    g1, g2, g3, g4, g5, g6, g7, g8, g_sq = [gy_ref[m] for m in range(9)]
    rx, ry, rz, sq = [tail_ref[d] for d in range(4)]
    inv = lax.rsqrt(1.0 + sq)
    ux, uy, uz = rx * inv, ry * inv, rz * inv
    gux = R3 * g1 + R15 * (uy * g4 + uz * g7 + ux * g8) - R5 * (ux * g6)
    guy = R3 * g2 + R15 * (ux * g4 + uz * g5 - uy * g8) - R5 * (uy * g6)
    guz = R3 * g3 + R15 * (uy * g5 + ux * g7) + (2.0 * R5) * (uz * g6)
    twice = 2.0 * g_sq - (gux * rx + guy * ry + guz * rz) * (inv * inv * inv)
    g_edge = [gux * inv + twice * rx, guy * inv + twice * ry, guz * inv + twice * rz]
    edges = jnp.concatenate(g_edge, axis=0)
    hi = head(edges)
    edges48 = jnp.concatenate([hi, edges - hi], axis=0).astype(BF16)

    def reduced(rows):
        at = lax.broadcasted_iota(jnp.int32, (8, rows.shape[1]), 0)
        out = jnp.zeros((8, rows.shape[1]), F32)
        for d in range(3):
            out = jnp.where(at == d, jnp.sum(rows[8 * d:8 * d + 8], axis=0, keepdims=True), out)
        return out

    away = dot(edges48, oh_ref[SL:EXT, :], NT)
    away = reduced(away[0:24] + away[24:48])
    fsend[0] = away[:, 0:128]
    fsend[1] = away[:, 128:256]
    lasts = [copy(fsend.at[f // 2], frecv.at[f], 14 + f, (xm, xp, ym, yp)[f]) for f in range(4)]
    for item in lasts:
        item.start()
    own = dot(edges48, oh_ref[0:SL, :], NT)
    own = own[0:24] + own[24:48]
    for k in range(NE):
        own = own - edges[:, k * SL:(k + 1) * SL]
    own = reduced(own)
    for item in lasts:
        item.wait()
    back8 = jnp.concatenate([jnp.where(low, frecv[0], frecv[1]), jnp.where(low, frecv[2], frecv[3])], axis=1)
    own = own + fold3(dot(stack3(back8), soh_ref[...], NT))
    force_out[...] = -own[0:3, :]
    for item in shares:
        item.wait()
    both = jnp.sum(column[...], axis=0)
    total = jnp.sum(jnp.where(low1, both, 0.0), axis=1, keepdims=True)
    number = jnp.sum(jnp.where(low1, 0.0, both), axis=1, keepdims=True)
    energy_out[...] = jnp.broadcast_to(total / number, (8, 128))


def shards(old_pos, old_species, block_dest, block_count, send_list, neighbours, embed, atom_ref,
           w_up, gammas, w_rad, w_mix, readout):
    vmem = pl.BlockSpec(memory_space=pltpu.VMEM)
    forces, energy = pl.pallas_call(
        body,
        name="potential",
        out_shape=(jax.ShapeDtypeStruct((3, SL), F32), jax.ShapeDtypeStruct((8, 128), F32)),
        in_specs=[pl.BlockSpec(memory_space=pltpu.HBM)] * 13,
        out_specs=(vmem, vmem),
        scratch_shapes=[
            pltpu.VMEM((3, 2 * BLK), F32),
            pltpu.VMEM((2 * BLK,), jnp.int32),
            pltpu.SMEM((1, 2), jnp.int32),
            pltpu.SMEM((2,), jnp.int32),
            pltpu.VMEM((4, GH), jnp.int32),
            pltpu.VMEM((NE, SL), jnp.int32),
            pltpu.VMEM((5, C), F32),
            pltpu.SMEM((5,), F32),
            pltpu.VMEM((2, C, C), F32),
            pltpu.SMEM((2, 8), F32),
            pltpu.VMEM((2, 8, 3 * C), F32),
            pltpu.VMEM((2, C, C), F32),
            pltpu.VMEM((2, C), F32),
            pltpu.VMEM((8, 2 * BLK), F32),
            pltpu.VMEM((2, 8, BLK), F32),
            pltpu.VMEM((2, 8, BLK), F32),
            pltpu.VMEM((8, SL), F32),
            pltpu.VMEM((4, 8, E), F32),
            pltpu.VMEM((2, 8, 128), F32),
            pltpu.VMEM((4, 8, 128), F32),
            pltpu.VMEM((8, C), F32),
            pltpu.VMEM((EXT, E), BF16),
            pltpu.VMEM((SL, NG), BF16),
            pltpu.VMEM((8, 8, E), F32),
            pltpu.VMEM((5, 8, E), F32),
            pltpu.VMEM((40, 9 * SL), F32),
            pltpu.VMEM((3, C, E), F32),
            pltpu.VMEM((3, C, E), F32),
            pltpu.VMEM((C, E), F32),
            pltpu.VMEM((C, E), F32),
            pltpu.VMEM((8, C, SL), F32),
            pltpu.VMEM((8, C, SL), F32),
            pltpu.VMEM((C, SL), F32),
            pltpu.VMEM((C, SL), F32),
            pltpu.VMEM((9, 40, SL), F32),
            pltpu.VMEM((2, C, E), F32),
            pltpu.VMEM((NG, C), F32),
            pltpu.VMEM((NG, C), F32),
            pltpu.VMEM((NG, C), F32),
            pltpu.VMEM((NG, C), F32),
            pltpu.VMEM((2, 8, 128), F32),
            pltpu.VMEM((4, 8, 128), F32),
            pltpu.VMEM((9, 8, E), F32),
            pltpu.VMEM((16, 1, 128), F32),
            pltpu.VMEM((32, 1, 128), F32),
            pltpu.SemaphoreType.DMA((13,)),
            pltpu.SemaphoreType.REGULAR,
            pltpu.SemaphoreType.DMA((64,)),
            pltpu.SemaphoreType.DMA((64,)),
        ],
        compiler_params=pltpu.CompilerParams(collective_id=0, has_side_effects=True, vmem_limit_bytes=40 * 1024 * 1024),
    )(*[pltpu.with_memory_space_constraint(x, pltpu.HBM) for x in (
        old_pos, old_species, block_dest.T, block_count, send_list, neighbours, embed, atom_ref,
        w_up, gammas, w_rad, w_mix, readout)])
    return forces, energy[0, 0]


def solution(mesh):
    both = ("gx", "yz")
    return jax.shard_map(
        shards,
        mesh=mesh,
        in_specs=(
            P(None, both), P(both), P(both, None), P(both), P(both, None), P(None, both),
            P(), P(), P(), P(), P(), P(), P(),
        ),
        out_specs=(P(None, both), P()),
        check_vma=False,
    )
```
